128 devices in a mesh: ctx: 32 (over y, z, core), mp: 4 (over x).
Axes of the slice: x: 4, y: 4, z: 4, core: 2. Of those that a mesh axis runs over, the one named last changes fastest.
Arguments:
- queries: bfloat16 [16384, 4096], P('ctx', 'mp'), may hold values from -15 to 15
- keys: bfloat16 [16384, 2048], P('ctx', 'mp'), may hold values from -15 to 15
- values: bfloat16 [16384, 2048], P('ctx', 'mp'), may hold values from -6 to 6
- grad_out: bfloat16 [16384, 4096], P(('ctx', 'mp')), may hold values from -6 to 6
- band_mask: int32 [128, 9], replicated, may hold values from 0 to 1, as said below
- segment_ids: int32 [16384], replicated, may hold values from 0 to 15, never falling along the last dimension, each value on 1 to 4096 neighbouring positions
Outputs:
- attn_out: bfloat16 [16384, 4096], P(('ctx', 'mp'))
- grad_queries: bfloat16 [16384, 4096], P('ctx', 'mp')
- grad_keys: bfloat16 [16384, 2048], P('ctx', 'mp')
- grad_values: bfloat16 [16384, 2048], P('ctx', 'mp')
The draws below stay inside these ranges and needn't reach their ends.
Inputs may be any that keep to these rules, and one draw needn't show every extreme that they name: band_mask[b, o] is 1 when query block b may see the key block o blocks before it; offset 0 is always 1. `segment_ids`: segment numbers never fall along the sequence.
All inputs are finite; a program needn't handle non-finite values.
Results may differ from the reference program's by a relative error of at most 0.03.
Values may be sent and summed in bfloat16 or wider, within the bound.
A program may use at most 128 MiB of HBM per device.

```python
import math
import jax
import jax.numpy as jnp
import numpy as np
from jax import lax

Q_HEADS = 32
KV_HEADS = 16
HEAD = 128
WINDOW = 1024
BLOCK = 128
TOKENS = 16384
NBAND = 9
NQB = 128
SEG_COUNT = 16
SEG_MOST = 4096


def paired_fields(key):
    query_base = jax.random.normal(jax.random.fold_in(key, 11), (TOKENS, Q_HEADS, HEAD), jnp.float32)
    key_base = jax.random.normal(jax.random.fold_in(key, 12), (TOKENS, KV_HEADS, HEAD), jnp.float32)
    query_base = jnp.clip(query_base, -15.0, 15.0)
    key_base = jnp.clip(key_base, -15.0, 15.0)
    return (query_base.reshape(TOKENS, Q_HEADS * HEAD), key_base.reshape(TOKENS, KV_HEADS * HEAD))


def draw_queries(key, part):
    return paired_fields(key)[0].astype(jnp.bfloat16)


def draw_keys(key, part):
    return paired_fields(key)[1].astype(jnp.bfloat16)


def draw_band_mask(key, part):
    bits = (jax.random.randint(key, (NQB, NBAND), 0, 10) < 7).astype(jnp.int32)
    return bits.at[:, 0].set(1)


def block_levels(stream_key, dims, pieces, smallest, largest):
    level, own = 1.0, jax.random.fold_in(stream_key, 6)
    for axis_at, parts in pieces:
        steps = jnp.exp(jax.random.uniform(jax.random.fold_in(own, axis_at), (parts,), jnp.float32, smallest / len(pieces), largest / len(pieces)))
        level = level * jnp.repeat(steps, dims[axis_at] // parts).reshape([-1 if axis == axis_at else 1 for axis in range(len(dims))])
    return level


def profile(number_of, total, limit, skew):
    portions = [(1 << 20) // math.isqrt(standing ** skew) + 1 for standing in range(2, number_of + 1)]
    surplus, given = total - limit - (number_of - 1), [1] * (number_of - 1)
    while surplus > 0:
        movable = [i for i in range(number_of - 1) if given[i] < limit]
        whole, budget = sum([portions[i] for i in movable]), surplus
        for i in movable:
            more = min(limit - given[i], max(1, budget * portions[i] // whole), surplus)
            given[i] = given[i] + more
            surplus = surplus - more
    return np.array([limit] + given)


def uneven_parts(stream_key, number_of, total, most, slope):
    if number_of == 2:
        one = jax.random.randint(stream_key, (), max(1, total - most), min(most, total - 1) + 1)
        return jnp.stack([one, total - one])
    sizes = jnp.asarray(profile(number_of, total, most, slope), jnp.int32)
    couples = (number_of - 1) // 2
    donor, receiver = sizes[1:1 + 2 * couples:2], sizes[2:2 + 2 * couples:2]
    room = jnp.minimum(donor - 1, most - receiver)
    passed = jax.random.randint(jax.random.fold_in(stream_key, 1), (couples,), 0, 1 << 20) % (room + 1)
    sizes = sizes.at[1:1 + 2 * couples:2].set(donor - passed).at[2:2 + 2 * couples:2].set(receiver + passed)
    return sizes[jax.random.permutation(jax.random.fold_in(stream_key, 2), number_of)]


def normal_values(key, extent, spread, most, shards=(), held_as=jnp.bfloat16):
    loudness = block_levels(key, extent, shards, -0.22, 0.18) if shards else 1.0
    result = jax.random.normal(key, extent, jnp.float32) * spread * loudness
    return jnp.minimum(jnp.maximum(result, -most), most).astype(held_as)


def setup_inputs(seed: int = 0) -> dict:
    seeds = jax.random.split(jax.random.key(seed), 7)
    queries = draw_queries(jax.random.fold_in(seeds[6], 71), 0)
    keys = draw_keys(jax.random.fold_in(seeds[6], 71), 0)
    values = normal_values(seeds[2], (TOKENS, KV_HEADS * HEAD), 1.0, 6.0, ((0, 32), (1, 4)))
    grad_out = normal_values(seeds[3], (TOKENS, Q_HEADS * HEAD), 1.0, 6.0, ((0, 128),))
    band_mask = draw_band_mask(jax.random.fold_in(seeds[6], 71), 0)
    segment_ids = jnp.searchsorted(jnp.cumsum(uneven_parts(seeds[5], SEG_COUNT, TOKENS, SEG_MOST, 2)), jnp.arange(TOKENS), side="right").astype(jnp.int32)
    return dict(queries=queries, keys=keys, values=values, grad_out=grad_out, band_mask=band_mask, segment_ids=segment_ids)


ATTN_SCALE = 168.0 ** -0.5
NEG_FILL = -1e30


def block_mask(seg_query, seg_key, band_row):
    rows_query = seg_query.shape[0]
    width_keys = seg_key.shape[0]
    distance = WINDOW + jnp.arange(rows_query)[:, None] - jnp.arange(width_keys)[None, :]
    allowed = jnp.repeat(band_row[::-1], BLOCK)
    return (distance >= 0) & (distance < WINDOW) & (seg_query[:, None] == seg_key[None, :]) & (allowed[None, :] == 1)


def reference(queries, keys, values, grad_out, band_mask, segment_ids):
    q_per_kv = Q_HEADS // KV_HEADS
    span_keys = WINDOW + BLOCK
    block_total = TOKENS // BLOCK
    key_pad = jnp.concatenate([jnp.zeros((WINDOW, KV_HEADS * HEAD), keys.dtype), keys]).reshape(TOKENS + WINDOW, KV_HEADS, HEAD)
    value_pad = jnp.concatenate([jnp.zeros((WINDOW, KV_HEADS * HEAD), values.dtype), values]).reshape(TOKENS + WINDOW, KV_HEADS, HEAD)
    seg_padded = jnp.concatenate([jnp.full((WINDOW,), -1, jnp.int32), segment_ids.astype(jnp.int32)])

    def step(carry, block_idx):
        key_grad, value_grad = carry
        start = (block_idx * BLOCK).astype(jnp.int32)
        query_blk = lax.dynamic_slice_in_dim(queries, start, BLOCK, 0).reshape(BLOCK, KV_HEADS, q_per_kv, HEAD).astype(jnp.float32)
        key_slab = lax.dynamic_slice_in_dim(key_pad, start, span_keys, 0).astype(jnp.float32)
        value_slab = lax.dynamic_slice_in_dim(value_pad, start, span_keys, 0).astype(jnp.float32)
        seg_query = lax.dynamic_slice_in_dim(segment_ids.astype(jnp.int32), start, BLOCK, 0)
        seg_key = lax.dynamic_slice_in_dim(seg_padded, start, span_keys, 0)
        band_row = lax.dynamic_index_in_dim(band_mask, block_idx, 0, keepdims=False)
        valid = block_mask(seg_query, seg_key, band_row)
        scores = jnp.einsum("qkgd,skd->kgqs", query_blk, key_slab) * ATTN_SCALE
        scores = jnp.where(valid, scores, NEG_FILL)
        row_max = jnp.max(scores, axis=-1, keepdims=True)
        log_norm = row_max + jnp.log(jnp.sum(jnp.exp(scores - row_max), axis=-1, keepdims=True))
        prob_bf = jnp.exp(scores - log_norm).astype(jnp.bfloat16)
        prob_wide = prob_bf.astype(jnp.float32)
        attended = jnp.einsum("kgqs,skd->qkgd", prob_wide, value_slab).astype(jnp.bfloat16)
        grad_blk = lax.dynamic_slice_in_dim(grad_out, start, BLOCK, 0).reshape(BLOCK, KV_HEADS, q_per_kv, HEAD).astype(jnp.float32)
        delta = jnp.sum(grad_blk * attended.astype(jnp.float32), axis=-1).transpose(1, 2, 0)[..., None]
        value_part = jnp.einsum("kgqs,qkgd->skd", prob_wide, grad_blk)
        grad_prob = jnp.einsum("qkgd,skd->kgqs", grad_blk, value_slab)
        grad_score = (prob_wide * (grad_prob - delta)).astype(jnp.bfloat16).astype(jnp.float32)
        grad_query = (jnp.einsum("kgqs,skd->qkgd", grad_score, key_slab) * ATTN_SCALE).astype(jnp.bfloat16)
        key_part = jnp.einsum("kgqs,qkgd->skd", grad_score, query_blk) * ATTN_SCALE
        key_grad = lax.dynamic_update_slice_in_dim(key_grad, lax.dynamic_slice_in_dim(key_grad, start, span_keys, 0) + key_part, start, 0)
        value_grad = lax.dynamic_update_slice_in_dim(value_grad, lax.dynamic_slice_in_dim(value_grad, start, span_keys, 0) + value_part, start, 0)
        return (key_grad, value_grad), (attended.reshape(BLOCK, Q_HEADS * HEAD), grad_query.reshape(BLOCK, Q_HEADS * HEAD))

    zeros = jnp.zeros((TOKENS + WINDOW, KV_HEADS, HEAD), jnp.float32)
    (key_grad, value_grad), (attended_all, grad_all) = lax.scan(step, (zeros, zeros), jnp.arange(block_total, dtype=jnp.int32))
    attn_out = attended_all.reshape(TOKENS, Q_HEADS * HEAD)
    grad_queries = grad_all.reshape(TOKENS, Q_HEADS * HEAD)
    grad_keys = key_grad[WINDOW:].reshape(TOKENS, KV_HEADS * HEAD).astype(jnp.bfloat16)
    grad_values = value_grad[WINDOW:].reshape(TOKENS, KV_HEADS * HEAD).astype(jnp.bfloat16)
    return (attn_out, grad_queries, grad_keys, grad_values)
```

```python
import math

import jax
import jax.numpy as jnp
from jax import lax
from jax.experimental import pallas as pl
from jax.experimental.pallas import tpu as pltpu
from jax.sharding import PartitionSpec as P

HEAD = 128
BLOCK = 128
WINDOW = 1024
CHIPS = 16
X = 4
SPAN = WINDOW + BLOCK
TILE = 384
ATTN_SCALE = 168.0 ** (-0.5)
EXP2_SCALE = ATTN_SCALE * math.log2(math.e)
NEG_FILL = -1e30
FAR = 1 << 20

MESH = pl.DeviceIdType.MESH
F32, BF16 = jnp.float32, jnp.bfloat16
NT = (((1,), (1,)), ((), ()))
NN = (((1,), (0,)), ((), ()))


def dot(a, b, dims):
    return lax.dot_general(a, b, dims, preferred_element_type=F32)


def unit(a, p, qs, gs, kx, vx, kt, vt, low, out, dq, dk, dv, s_scr, e_scr, d_scr):
    start = pl.multiple_of(p * BLOCK, BLOCK)
    q = qs[a, p]
    top = jnp.full((8, 2 * BLOCK), NEG_FILL, F32)
    row = lax.broadcasted_iota(jnp.int32, (BLOCK, 2 * BLOCK), 0)
    col = lax.broadcasted_iota(jnp.int32, (BLOCK, 2 * BLOCK), 1) % BLOCK
    for t in range(SPAN // TILE):
        s = dot(kx[a, pl.ds(start + t * TILE, TILE), :], q, NT)
        for u in range(TILE // BLOCK):
            tile = t * (TILE // BLOCK) + u
            ok = row >= low[tile, pl.ds(p, 1), :]
            if tile == WINDOW // BLOCK:
                ok = ok & (row <= col)
            part = jnp.where(ok, s[u * BLOCK : (u + 1) * BLOCK], NEG_FILL)
            s_scr[tile * BLOCK : (tile + 1) * BLOCK, :] = part
            top = jnp.maximum(top, jnp.max(part.reshape(BLOCK // 8, 8, 2 * BLOCK), axis=0))
    top = jnp.max(top, axis=0, keepdims=True)
    total = jnp.zeros((8, 2 * BLOCK), F32)
    for tile in range(SPAN // BLOCK):
        rows = slice(tile * BLOCK, (tile + 1) * BLOCK)
        e = jnp.exp2((s_scr[rows, :] - top) * EXP2_SCALE)
        total = total + jnp.sum(e.reshape(BLOCK // 8, 8, 2 * BLOCK), axis=0)
        e_scr[rows, :] = e.astype(BF16)
    inv = 1.0 / jnp.sum(total, axis=0, keepdims=True)
    window = pl.ds(start, SPAN)
    o_t = (dot(vt[a, :, window], e_scr[...], NN) * inv).astype(BF16)
    g_t = (gs[a, p].T.astype(F32) * inv).astype(BF16)
    delta = jnp.sum(g_t.astype(F32) * o_t.astype(F32), axis=0, keepdims=True)
    out[a, p] = o_t.T
    for t in range(SPAN // TILE):
        rows = slice(t * TILE, (t + 1) * TILE)
        key_rows = pl.ds(start + t * TILE, TILE)
        e = e_scr[rows, :]
        ds = (e.astype(F32) * (dot(vx[a, key_rows, :], g_t, NN) - delta)).astype(BF16)
        d_scr[rows, :] = ds
        dv[key_rows, :] += dot(e, g_t, NT)
        dk[key_rows, :] += dot(ds, q, NN)
    dq[a, p] = (dot(kt[a, :, window], d_scr[...], NN) * ATTN_SCALE).astype(BF16).T


def kernel(
    q_ref, k_ref, v_ref, g_ref, band_ref, seg_ref,
    attn_ref, dq_ref, dk_ref, dv_ref,
    qs, gs, kx, vx, kt, vt, low, out, dqs, dk, dv, s_scr, e_scr, d_scr,
    hk, hv, pk, pv, rk, rv, lk, lv,
    send, q_in, k_in, v_in, hk_in, hv_in, g_in, o_in, dq_in, rk_in, rv_in, lk_in, lv_in,
):
    me, x = lax.axis_index("ctx"), lax.axis_index("mp")
    chip, core = me // 2, me % 2
    after, before = lax.rem(chip + 1, CHIPS), lax.rem(chip + CHIPS - 1, CHIPS)
    mate = 2 * chip + 1 - core

    barrier = pltpu.get_barrier_semaphore()
    for step in range(1, 2 * X):
        peer = lax.rem(core * X + x + step, 2 * X)
        pl.semaphore_signal(
            barrier, inc=1, device_id=(2 * chip + peer // X, peer % X), device_id_type=MESH
        )
    for other in (after, before):
        for c in range(2):
            pl.semaphore_signal(barrier, inc=1, device_id=(2 * other + c, x), device_id_type=MESH)
    pl.semaphore_wait(barrier, 2 * X - 1 + 4)

    def push(src, dst, send_at, recv, to):
        pltpu.make_async_remote_copy(
            src_ref=src, dst_ref=dst, send_sem=send.at[send_at], recv_sem=recv,
            device_id=to, device_id_type=MESH,
        ).start()

    def wait(ref, sem):
        pltpu.make_async_copy(ref, ref, sem).wait()

    own_rows = pl.ds(pl.multiple_of(core * 512, 512), 512)
    local_rows = pl.ds(pl.multiple_of(WINDOW + core * 512, 512), 512)
    my_block = core * X + x

    def columns(head):
        return pl.ds(pl.multiple_of(head * HEAD, HEAD), HEAD)

    for a in range(2):
        for ref, buf, at, sem in ((k_ref, kx, 0, hk_in), (v_ref, vx, 1, hv_in)):
            for c in range(2):
                push(
                    ref.at[:, (2 * c + a) * HEAD : (2 * c + a + 1) * HEAD],
                    buf.at[a, own_rows, :], at, sem.at[a], (2 * after + c, x),
                )
        theirs, mine = 2 * (1 - core) + a, 2 * core + a
        for ref, buf, at, sem in ((k_ref, kx, 2, k_in), (v_ref, vx, 3, v_in)):
            push(ref.at[:, columns(theirs)], buf.at[a, local_rows, :], at, sem.at[a], (mate, x))
            pltpu.make_async_copy(ref.at[:, columns(mine)], buf.at[a, local_rows, :], sem.at[a]).start()
        for g in range(2):
            rows = slice(g * BLOCK, (g + 1) * BLOCK)
            dst = qs.at[a, pl.ds(core * X, X), rows, :]
            push(q_ref.at[:, :, columns(2 * theirs + g)], dst, 4, q_in.at[a], (mate, x))
            pltpu.make_async_copy(q_ref.at[:, :, columns(2 * mine + g)], dst, q_in.at[a]).start()
            dst = gs.at[a, my_block, rows, :]
            for step in range(1, 2 * X):
                peer = lax.rem(my_block + step, 2 * X)
                c, to_x = peer // X, peer % X
                push(
                    g_ref.at[:, columns(to_x * 8 + c * 4 + 2 * a + g)], dst, 5, g_in.at[a],
                    (2 * chip + c, to_x),
                )
            pltpu.make_async_copy(
                g_ref.at[:, columns(x * 8 + core * 4 + 2 * a + g)], dst, g_in.at[a]
            ).start()

    seg = seg_ref[pl.ds(pl.multiple_of(8 * chip, 8), 8), :]
    every = seg_ref[...]
    begin = jnp.zeros((8, BLOCK), jnp.int32)
    for s in range(1, 16):
        count = jnp.sum((every < s).astype(jnp.int32), axis=0, keepdims=True)
        count = jnp.sum(count, axis=1, keepdims=True)
        begin = jnp.maximum(begin, jnp.where(seg >= s, count, 0))
    block = lax.broadcasted_iota(jnp.int32, (8, BLOCK), 0)
    lane = lax.broadcasted_iota(jnp.int32, (8, BLOCK), 1)
    first = jnp.maximum(begin - (chip - 1) * WINDOW, block * BLOCK + lane + 1)
    bands = band_ref[pl.ds(pl.multiple_of(8 * chip, 8), 8), :]
    for tile in range(SPAN // BLOCK):
        o = WINDOW // BLOCK - tile
        value = first - (block + tile) * BLOCK + (1 - bands[:, o : o + 1]) * FAR
        low[tile] = jnp.concatenate([value, value], axis=1)

    def loop(i, carry):
        a, p = i // 8, i % 8

        @pl.when(p == 0)
        def _():
            wait(kx.at[a, WINDOW:, :], k_in.at[a])
            wait(vx.at[a, WINDOW:, :], v_in.at[a])
            wait(kx.at[a, :WINDOW, :], hk_in.at[a])
            wait(vx.at[a, :WINDOW, :], hv_in.at[a])

            def turn(b, c):
                rows = pl.ds(pl.multiple_of(b * BLOCK, BLOCK), BLOCK)
                kt[a, :, rows] = kx[a, rows, :].T
                vt[a, :, rows] = vx[a, rows, :].T
                return c

            lax.fori_loop(0, 16, turn, 0)
            dk[...] = jnp.zeros_like(dk)
            dv[...] = jnp.zeros_like(dv)
            wait(qs.at[a], q_in.at[a])
            wait(gs.at[a], g_in.at[a])

        unit(a, p, qs, gs, kx, vx, kt, vt, low, out, dqs, dk, dv, s_scr, e_scr, d_scr)

        head = 2 * core + a
        rows = pl.ds(pl.multiple_of(p * BLOCK, BLOCK), BLOCK)
        hk[a, p] = (dk[rows, :] * ATTN_SCALE).astype(BF16)
        hv[a, p] = dv[rows, :].astype(BF16)
        at_rows = pl.ds(pl.multiple_of((p % 4) * BLOCK, BLOCK), BLOCK)
        to = (2 * before + p // 4, x)
        push(hk.at[a, p], rk.at[head, at_rows, :], 6, rk_in.at[head], to)
        push(hv.at[a, p], rv.at[head, at_rows, :], 7, rv_in.at[head], to)
        for g in range(2):
            part = slice(g * BLOCK, (g + 1) * BLOCK)
            src = out.at[a, p, part, :]
            dst = attn_ref.at[:, columns(x * 8 + core * 4 + 2 * a + g)]

            @pl.when(p == my_block)
            def _():
                pltpu.make_async_copy(src, dst, o_in).start()

            @pl.when(p != my_block)
            def _():
                push(src, dst, 8, o_in, (2 * chip + p // 4, p % 4))

            src2 = dqs.at[a, p, part, :]
            dst2 = dq_ref.at[p % 4, :, columns(2 * head + g)]

            @pl.when(p // 4 == core)
            def _():
                pltpu.make_async_copy(src2, dst2, dq_in).start()

            @pl.when(p // 4 != core)
            def _():
                push(src2, dst2, 9, dq_in, (mate, x))

        @pl.when(p == 7)
        def _():
            theirs = pl.ds(pl.multiple_of(WINDOW + (1 - core) * 512, 512), 512)
            pk[a] = (dk[theirs, :] * ATTN_SCALE).astype(BF16)
            pv[a] = dv[theirs, :].astype(BF16)
            push(pk.at[a], lk.at[head], 10, lk_in.at[a], (mate, x))
            push(pv.at[a], lv.at[head], 11, lv_in.at[a], (mate, x))
            lk[head] = (dk[local_rows, :] * ATTN_SCALE).astype(BF16)
            lv[head] = dv[local_rows, :].astype(BF16)

        return carry

    lax.fori_loop(0, 16, loop, 0)

    for a in range(2):
        wait(lk.at[0], lk_in.at[a])
        wait(lv.at[0], lv_in.at[a])
    for h in range(4):
        cols = slice(h * HEAD, (h + 1) * HEAD)
        wait(rk.at[h], rk_in.at[h])
        wait(rv.at[h], rv_in.at[h])
        dk_ref[:, cols] = (lk[h].astype(F32) + rk[h].astype(F32)).astype(BF16)
        dv_ref[:, cols] = (lv[h].astype(F32) + rv[h].astype(F32)).astype(BF16)
    wait(attn_ref, o_in)
    wait(dq_ref, dq_in)
    wait(k_ref, send.at[0])
    wait(v_ref, send.at[1])
    wait(k_ref.at[:, : 2 * HEAD], send.at[2])
    wait(v_ref.at[:, : 2 * HEAD], send.at[3])
    wait(q_ref.at[:, :, : 4 * HEAD], send.at[4])
    wait(g_ref.at[:, : 28 * HEAD], send.at[5])
    wait(hk, send.at[6])
    wait(hv, send.at[7])
    wait(out.at[:, :7], send.at[8])
    wait(dqs.at[:, :4], send.at[9])
    wait(pk, send.at[10])
    wait(pv, send.at[11])


def body(queries, keys, values, grad_out, band_mask, segment_ids):
    hbm = pl.BlockSpec(memory_space=pl.ANY)
    vmem = pl.BlockSpec(memory_space=pltpu.VMEM)
    dma = pltpu.SemaphoreType.DMA
    attn, dq, dk, dv = pl.pallas_call(
        kernel,
        out_shape=(
            jax.ShapeDtypeStruct((128, 4096), BF16),
            jax.ShapeDtypeStruct((4, 128, 1024), BF16),
            jax.ShapeDtypeStruct((512, 512), BF16),
            jax.ShapeDtypeStruct((512, 512), BF16),
        ),
        in_specs=[hbm, hbm, hbm, hbm, vmem, vmem],
        out_specs=(hbm, hbm, vmem, vmem),
        scratch_shapes=[
            pltpu.VMEM((2, 8, 256, 128), BF16),
            pltpu.VMEM((2, 8, 256, 128), BF16),
            pltpu.VMEM((2, 2048, 128), BF16),
            pltpu.VMEM((2, 2048, 128), BF16),
            pltpu.VMEM((2, 128, 2048), BF16),
            pltpu.VMEM((2, 128, 2048), BF16),
            pltpu.VMEM((9, 8, 256), jnp.int32),
            pltpu.VMEM((2, 8, 256, 128), BF16),
            pltpu.VMEM((2, 8, 256, 128), BF16),
            pltpu.VMEM((2048, 128), F32),
            pltpu.VMEM((2048, 128), F32),
            pltpu.VMEM((SPAN, 256), F32),
            pltpu.VMEM((SPAN, 256), BF16),
            pltpu.VMEM((SPAN, 256), BF16),
            pltpu.VMEM((2, 8, 128, 128), BF16),
            pltpu.VMEM((2, 8, 128, 128), BF16),
            pltpu.VMEM((2, 512, 128), BF16),
            pltpu.VMEM((2, 512, 128), BF16),
            pltpu.VMEM((4, 512, 128), BF16),
            pltpu.VMEM((4, 512, 128), BF16),
            pltpu.VMEM((4, 512, 128), BF16),
            pltpu.VMEM((4, 512, 128), BF16),
            dma((12,)),
            dma((2,)), dma((2,)), dma((2,)), dma((2,)), dma((2,)), dma((2,)),
            dma(()), dma(()),
            dma((4,)), dma((4,)), dma((2,)), dma((2,)),
        ],
        compiler_params=pltpu.CompilerParams(
            collective_id=0, has_side_effects=True, vmem_limit_bytes=48 << 20
        ),
    )(queries.reshape(4, 128, 1024), keys, values, grad_out, band_mask, segment_ids.reshape(128, 128))
    return attn, dq.reshape(512, 1024), dk, dv


def solution(mesh):
    placed = (P("ctx", "mp"), P("ctx", "mp"), P("ctx", "mp"), P(("ctx", "mp"), None), P(), P())
    return jax.shard_map(
        body,
        mesh=mesh,
        in_specs=placed,
        out_specs=(P(("ctx", "mp"), None), P("ctx", "mp"), P("ctx", "mp"), P("ctx", "mp")),
        check_vma=False,
    )
```

```python
import math

import jax
import jax.numpy as jnp
from jax import lax
from jax.experimental import pallas as pl
from jax.experimental.pallas import tpu as pltpu
from jax.sharding import PartitionSpec as P

HEAD = 128
BLOCK = 128
WINDOW = 1024
CHIPS = 16
X = 4
SPAN = WINDOW + BLOCK
TILE = 384
ATTN_SCALE = 168.0 ** (-0.5)
EXP2_SCALE = ATTN_SCALE * math.log2(math.e)
NEG_FILL = -1e30
FAR = 1 << 20

MESH = pl.DeviceIdType.MESH
F32, BF16 = jnp.float32, jnp.bfloat16
NT = (((1,), (1,)), ((), ()))
NN = (((1,), (0,)), ((), ()))


def dot(a, b, dims):
    return lax.dot_general(a, b, dims, preferred_element_type=F32)


def scores(a, p, qs, kx, low, s_scr, e_scr, inv_scr):
    start = pl.multiple_of(p * BLOCK, BLOCK)
    q = qs[a, p]
    top = jnp.full((8, 2 * BLOCK), NEG_FILL, F32)
    row = lax.broadcasted_iota(jnp.int32, (BLOCK, 2 * BLOCK), 0)
    col = lax.broadcasted_iota(jnp.int32, (BLOCK, 2 * BLOCK), 1) % BLOCK
    for t in range(SPAN // TILE):
        s = dot(kx[a, pl.ds(start + t * TILE, TILE), :], q, NT)
        for u in range(TILE // BLOCK):
            tile = t * (TILE // BLOCK) + u
            ok = row >= low[tile, pl.ds(p, 1), :]
            if tile == WINDOW // BLOCK:
                ok = ok & (row <= col)
            part = jnp.where(ok, s[u * BLOCK : (u + 1) * BLOCK], NEG_FILL)
            s_scr[tile * BLOCK : (tile + 1) * BLOCK, :] = part
            top = jnp.maximum(top, jnp.max(part.reshape(BLOCK // 8, 8, 2 * BLOCK), axis=0))
        yield
    top = jnp.max(top, axis=0, keepdims=True)
    total = jnp.zeros((8, 2 * BLOCK), F32)
    for tile in range(SPAN // BLOCK):
        rows = slice(tile * BLOCK, (tile + 1) * BLOCK)
        e = jnp.exp2((s_scr[rows, :] - top) * EXP2_SCALE)
        total = total + jnp.sum(e.reshape(BLOCK // 8, 8, 2 * BLOCK), axis=0)
        e_scr[rows, :] = e.astype(BF16)
        yield
    inv = 1.0 / jnp.sum(total, axis=0, keepdims=True)
    inv_scr[...] = jnp.broadcast_to(inv, (8, 2 * BLOCK))


def gradients(a, p, qs, gs, kx, vx, kt, vt, out, dq, dk, dv, e_scr, inv_scr, d_scr):
    start = pl.multiple_of(p * BLOCK, BLOCK)
    window = pl.ds(start, SPAN)
    q = qs[a, p]
    inv = inv_scr[0:1, :]
    g_t = (gs[a, p].T.astype(F32) * inv).astype(BF16)
    o_t = (dot(vt[a, :, window], e_scr[...], NN) * inv).astype(BF16)
    delta = jnp.sum(g_t.astype(F32) * o_t.astype(F32), axis=0, keepdims=True)
    out[a, p] = o_t.T
    yield
    for t in range(SPAN // TILE):
        rows = slice(t * TILE, (t + 1) * TILE)
        key_rows = pl.ds(start + t * TILE, TILE)
        e = e_scr[rows, :]
        ds = (e.astype(F32) * (dot(vx[a, key_rows, :], g_t, NN) - delta)).astype(BF16)
        d_scr[rows, :] = ds
        yield
        dv[a, key_rows, :] += dot(e, g_t, NT)
        dk[a, key_rows, :] += dot(ds, q, NN)
        yield
    dq[a, p] = (dot(kt[a, :, window], d_scr[...], NN) * ATTN_SCALE).astype(BF16).T


def interleave(first, second):
    live = True
    while live:
        live = False
        for chunks, times in ((first, 1), (second, 3)):
            for _ in range(times):
                live = next(chunks, chunks) is not chunks or live


def kernel(
    q_ref, k_ref, v_ref, g_ref, band_ref, seg_ref,
    attn_ref, dq_ref, lk, lv, rk, rv,
    qs, gs, kx, vx, kt, vt, low, out, dqs, dk, dv, s_scr, e_0, e_1, inv_0, inv_1, d_scr,
    hk, hv, pk, pv, seg_v, band_v, band_t,
    send, q_in, k_in, v_in, hk_in, hv_in, g_in, o_in, dq_in, rk_in, rv_in, lk_in, lv_in, seg_in, band_in,
):
    me, x = lax.axis_index("ctx"), lax.axis_index("mp")
    chip, core = me // 2, me % 2
    after, before = lax.rem(chip + 1, CHIPS), lax.rem(chip + CHIPS - 1, CHIPS)
    mate = 2 * chip + 1 - core

    barrier = pltpu.get_barrier_semaphore()
    for step in range(1, 2 * X):
        peer = lax.rem(core * X + x + step, 2 * X)
        pl.semaphore_signal(
            barrier, inc=1, device_id=(2 * chip + peer // X, peer % X), device_id_type=MESH
        )
    for other in (after, before):
        for c in range(2):
            pl.semaphore_signal(barrier, inc=1, device_id=(2 * other + c, x), device_id_type=MESH)

    def push(src, dst, send_at, recv, to):
        pltpu.make_async_remote_copy(
            src_ref=src, dst_ref=dst, send_sem=send.at[send_at], recv_sem=recv,
            device_id=to, device_id_type=MESH,
        ).start()

    def wait(ref, sem):
        pltpu.make_async_copy(ref, ref, sem).wait()

    own_rows = pl.ds(pl.multiple_of(core * 512, 512), 512)
    local_rows = pl.ds(pl.multiple_of(WINDOW + core * 512, 512), 512)
    my_block = core * X + x

    def columns(head):
        return pl.ds(pl.multiple_of(head * HEAD, HEAD), HEAD)

    pltpu.make_async_copy(seg_ref, seg_v, seg_in).start()
    pltpu.make_async_copy(band_ref, band_v, band_in).start()
    pl.semaphore_wait(barrier, 2 * X - 1 + 4)

    for a in range(2):
        for ref, buf, at, sem in ((k_ref, kx, 0, hk_in), (v_ref, vx, 1, hv_in)):
            for c in range(2):
                push(
                    ref.at[:, (2 * c + a) * HEAD : (2 * c + a + 1) * HEAD],
                    buf.at[a, own_rows, :], at, sem.at[a], (2 * after + c, x),
                )
        theirs, mine = 2 * (1 - core) + a, 2 * core + a
        for ref, buf, at, sem in ((k_ref, kx, 2, k_in), (v_ref, vx, 3, v_in)):
            push(ref.at[:, columns(theirs)], buf.at[a, local_rows, :], at, sem.at[a], (mate, x))
            pltpu.make_async_copy(ref.at[:, columns(mine)], buf.at[a, local_rows, :], sem.at[a]).start()
        for g in range(2):
            rows = slice(g * BLOCK, (g + 1) * BLOCK)
            dst = qs.at[a, pl.ds(core * X, X), rows, :]
            push(q_ref.at[:, :, columns(2 * theirs + g)], dst, 4, q_in.at[a], (mate, x))
            pltpu.make_async_copy(q_ref.at[:, :, columns(2 * mine + g)], dst, q_in.at[a]).start()
            dst = gs.at[a, my_block, rows, :]
            pltpu.make_async_copy(
                g_ref.at[:, columns(x * 8 + core * 4 + 2 * a + g)], dst, g_in.at[a]
            ).start()

            def spread(step, carry, dst=dst, a=a, g=g):
                peer = lax.rem(my_block + step, 2 * X)
                c, to_x = peer // X, peer % X
                push(
                    g_ref.at[:, columns(to_x * 8 + c * 4 + 2 * a + g)], dst, 5, g_in.at[a],
                    (2 * chip + c, to_x),
                )
                return carry

            lax.fori_loop(1, 2 * X, spread, 0)

    wait(seg_v, seg_in)
    wait(band_v, band_in)
    seg = seg_v[pl.ds(pl.multiple_of(8 * chip, 8), 8), :]
    every = seg_v[...]
    begin = jnp.zeros((8, BLOCK), jnp.int32)
    for s in range(1, 16):
        count = jnp.sum((every < s).astype(jnp.int32), axis=0, keepdims=True)
        count = jnp.sum(count, axis=1, keepdims=True)
        begin = jnp.maximum(begin, jnp.where(seg >= s, count, 0))
    block = lax.broadcasted_iota(jnp.int32, (8, BLOCK), 0)
    lane = lax.broadcasted_iota(jnp.int32, (8, BLOCK), 1)
    first = jnp.maximum(begin - (chip - 1) * WINDOW, block * BLOCK + lane + 1)
    bands = jnp.concatenate([band_v[...], jnp.zeros((7, 128), jnp.int32)], axis=0)
    band_t[...] = bands.T
    bands = band_t[pl.ds(pl.multiple_of(8 * chip, 8), 8), :]
    for tile in range(SPAN // BLOCK):
        o = WINDOW // BLOCK - tile
        value = first - (block + tile) * BLOCK + (1 - bands[:, o : o + 1]) * FAR
        low[tile] = jnp.concatenate([value, value], axis=1)

    def turn(a, b):
        rows = pl.ds(pl.multiple_of(b * BLOCK, BLOCK), BLOCK)
        kt[a, :, rows] = kx[a, rows, :].T
        vt[a, :, rows] = vx[a, rows, :].T

    def turn_local(i, carry):
        turn(i // 8, 8 + i % 8)
        return carry

    def turn_halo(i, carry):
        turn(carry, i)
        return carry

    def score_inputs(a):
        wait(kx.at[a, :WINDOW, :], hk_in.at[a])
        wait(vx.at[a, :WINDOW, :], hv_in.at[a])
        lax.fori_loop(0, 8, turn_halo, a)

    dk[...] = jnp.zeros_like(dk)
    dv[...] = jnp.zeros_like(dv)
    for a in range(2):
        wait(kx.at[a, WINDOW:, :], k_in.at[a])
        wait(vx.at[a, WINDOW:, :], v_in.at[a])
        wait(qs.at[a], q_in.at[a])
    lax.fori_loop(0, 16, turn_local, 0)
    e_scr, inv_scr = (e_0, e_1), (inv_0, inv_1)

    def score(i, slot):
        return scores(i // 8, i % 8, qs, kx, low, s_scr, e_scr[slot], inv_scr[slot])

    def grad(i, slot):
        return gradients(
            i // 8, i % 8, qs, gs, kx, vx, kt, vt, out, dqs, dk, dv, e_scr[slot], inv_scr[slot], d_scr
        )

    def deliver(i):
        a, p = i // 8, i % 8
        head = 2 * core + a
        rows = pl.ds(pl.multiple_of(p * BLOCK, BLOCK), BLOCK)
        hk[a, p] = (dk[a, rows, :] * ATTN_SCALE).astype(BF16)
        hv[a, p] = dv[a, rows, :].astype(BF16)
        at_rows = pl.ds(pl.multiple_of((p % 4) * BLOCK, BLOCK), BLOCK)
        to = (2 * before + p // 4, x)
        push(hk.at[a, p], rk.at[head, at_rows, :], 6, rk_in.at[head], to)
        push(hv.at[a, p], rv.at[head, at_rows, :], 7, rv_in.at[head], to)
        for g in range(2):
            part = slice(g * BLOCK, (g + 1) * BLOCK)
            src = out.at[a, p, part, :]
            dst = attn_ref.at[:, columns(x * 8 + core * 4 + 2 * a + g)]

            @pl.when(p == my_block)
            def _():
                pltpu.make_async_copy(src, dst, o_in).start()

            @pl.when(p != my_block)
            def _():
                push(src, dst, 8, o_in, (2 * chip + p // 4, p % 4))

            src2 = dqs.at[a, p, part, :]
            dst2 = dq_ref.at[p % 4, :, columns(2 * head + g)]

            @pl.when(p // 4 == core)
            def _():
                pltpu.make_async_copy(src2, dst2, dq_in).start()

            @pl.when(p // 4 != core)
            def _():
                push(src2, dst2, 9, dq_in, (mate, x))

        @pl.when(p == 7)
        def _():
            theirs = pl.ds(pl.multiple_of(WINDOW + (1 - core) * 512, 512), 512)
            pk[a] = (dk[a, theirs, :] * ATTN_SCALE).astype(BF16)
            pv[a] = dv[a, theirs, :].astype(BF16)
            push(pk.at[a], lk.at[head], 10, lk_in.at[a], (mate, x))
            push(pv.at[a], lv.at[head], 11, lv_in.at[a], (mate, x))
            lk[head] = (dk[a, local_rows, :] * ATTN_SCALE).astype(BF16)
            lv[head] = dv[a, local_rows, :].astype(BF16)

    score_inputs(0)
    for _ in score(0, 0):
        pass
    wait(gs.at[0], g_in.at[0])

    def loop(j, carry):
        interleave(grad(2 * j, 0), score(2 * j + 1, 1))
        deliver(2 * j)

        @pl.when(j == 3)
        def _():
            score_inputs(1)
            wait(gs.at[1], g_in.at[1])

        interleave(grad(2 * j + 1, 1), score(jnp.minimum(2 * j + 2, 15), 0))
        deliver(2 * j + 1)
        return carry

    lax.fori_loop(0, 8, loop, 0)

    for a in range(2):
        wait(lk.at[0], lk_in.at[a])
        wait(lv.at[0], lv_in.at[a])
    for h in range(4):
        wait(rk.at[h], rk_in.at[h])
        wait(rv.at[h], rv_in.at[h])
    wait(attn_ref, o_in)
    wait(dq_ref, dq_in)
    wait(k_ref, send.at[0])
    wait(v_ref, send.at[1])
    wait(k_ref.at[:, : 2 * HEAD], send.at[2])
    wait(v_ref.at[:, : 2 * HEAD], send.at[3])
    wait(q_ref.at[:, :, : 4 * HEAD], send.at[4])
    wait(g_ref.at[:, : 28 * HEAD], send.at[5])
    wait(hk, send.at[6])
    wait(hv, send.at[7])
    wait(out.at[:, :7], send.at[8])
    wait(dqs.at[:, :4], send.at[9])
    wait(pk, send.at[10])
    wait(pv, send.at[11])


def finish(attn_ref, dq_ref, lk, lv, rk, rv, attn_out, dq_out, dk_out, dv_out, dk, dv, sems):
    copies = [
        pltpu.make_async_copy(attn_ref, attn_out, sems.at[0]),
        pltpu.make_async_copy(dq_ref, dq_out, sems.at[1]),
        pltpu.make_async_copy(dk, dk_out, sems.at[2]),
        pltpu.make_async_copy(dv, dv_out, sems.at[3]),
    ]
    copies[0].start()
    copies[1].start()
    for ours, other, total, copy in ((lk, rk, dk, copies[2]), (lv, rv, dv, copies[3])):
        for h in range(4):
            cols = slice(h * HEAD, (h + 1) * HEAD)
            total[:, cols] = (ours[h].astype(F32) + other[h].astype(F32)).astype(BF16)
        copy.start()
    for copy in copies:
        copy.wait()


def body(queries, keys, values, grad_out, band_mask, segment_ids):
    hbm = pl.BlockSpec(memory_space=pltpu.HBM)
    anywhere = pl.BlockSpec(memory_space=pl.ANY)
    vmem = pl.BlockSpec(memory_space=pltpu.VMEM)
    dma = pltpu.SemaphoreType.DMA
    attn_shape = jax.ShapeDtypeStruct((128, 4096), BF16)
    dq_shape = jax.ShapeDtypeStruct((4, 128, 1024), BF16)
    part = jax.ShapeDtypeStruct((4, 512, 128), BF16)
    pieces = pl.pallas_call(
        kernel,
        out_shape=(attn_shape, dq_shape, part, part, part, part),
        in_specs=[hbm] * 6,
        out_specs=(anywhere, anywhere, vmem, vmem, vmem, vmem),
        scratch_shapes=[
            pltpu.VMEM((2, 8, 256, 128), BF16),
            pltpu.VMEM((2, 8, 256, 128), BF16),
            pltpu.VMEM((2, 2048, 128), BF16),
            pltpu.VMEM((2, 2048, 128), BF16),
            pltpu.VMEM((2, 128, 2048), BF16),
            pltpu.VMEM((2, 128, 2048), BF16),
            pltpu.VMEM((9, 8, 256), jnp.int32),
            pltpu.VMEM((2, 8, 256, 128), BF16),
            pltpu.VMEM((2, 8, 256, 128), BF16),
            pltpu.VMEM((2, 2048, 128), F32),
            pltpu.VMEM((2, 2048, 128), F32),
            pltpu.VMEM((SPAN, 256), F32),
            pltpu.VMEM((SPAN, 256), BF16),
            pltpu.VMEM((SPAN, 256), BF16),
            pltpu.VMEM((8, 256), F32),
            pltpu.VMEM((8, 256), F32),
            pltpu.VMEM((SPAN, 256), BF16),
            pltpu.VMEM((2, 8, 128, 128), BF16),
            pltpu.VMEM((2, 8, 128, 128), BF16),
            pltpu.VMEM((2, 512, 128), BF16),
            pltpu.VMEM((2, 512, 128), BF16),
            pltpu.VMEM((128, 128), jnp.int32),
            pltpu.VMEM((9, 128), jnp.int32),
            pltpu.VMEM((128, 16), jnp.int32),
            dma((12,)),
            dma((2,)), dma((2,)), dma((2,)), dma((2,)), dma((2,)), dma((2,)),
            dma(()), dma(()),
            dma((4,)), dma((4,)), dma((2,)), dma((2,)),
            dma(()), dma(()),
        ],
        compiler_params=pltpu.CompilerParams(
            collective_id=0, has_side_effects=True, vmem_limit_bytes=48 << 20
        ),
    )(
        *(
            pltpu.with_memory_space_constraint(array, pltpu.HBM)
            for array in (
                queries.reshape(4, 128, 1024), keys, values, grad_out,
                band_mask.T, segment_ids.reshape(128, 128),
            )
        )
    )
    grad = jax.ShapeDtypeStruct((512, 512), BF16)
    attn, dq, dk, dv = pl.pallas_call(
        finish,
        out_shape=(attn_shape, dq_shape, grad, grad),
        in_specs=[anywhere, anywhere, vmem, vmem, vmem, vmem],
        out_specs=(hbm,) * 4,
        scratch_shapes=[pltpu.VMEM((512, 512), BF16), pltpu.VMEM((512, 512), BF16), dma((4,))],
        compiler_params=pltpu.CompilerParams(vmem_limit_bytes=16 << 20),
    )(*pieces)
    return attn, dq.reshape(512, 1024), dk, dv


def solution(mesh):
    placed = (P("ctx", "mp"), P("ctx", "mp"), P("ctx", "mp"), P(("ctx", "mp"), None), P(), P())
    return jax.shard_map(
        body,
        mesh=mesh,
        in_specs=placed,
        out_specs=(P(("ctx", "mp"), None), P("ctx", "mp"), P("ctx", "mp"), P("ctx", "mp")),
        check_vma=False,
    )
```

```python
import math

import jax
import jax.numpy as jnp
from jax import lax
from jax.experimental import pallas as pl
from jax.experimental.pallas import tpu as pltpu
from jax.sharding import PartitionSpec as P

HEAD = 128
BLOCK = 128
WINDOW = 1024
CHIPS = 16
X = 4
SPAN = WINDOW + BLOCK
TILE = 384
ATTN_SCALE = 168.0 ** (-0.5)
EXP2_SCALE = ATTN_SCALE * math.log2(math.e)
NEG_FILL = -1e30
ORDER = ((0, 1), (1, 0))
FAR = 1 << 20

MESH = pl.DeviceIdType.MESH
F32, BF16 = jnp.float32, jnp.bfloat16
NT = (((1,), (1,)), ((), ()))
NN = (((1,), (0,)), ((), ()))


def dot(a, b, dims):
    return lax.dot_general(a, b, dims, preferred_element_type=F32)


def scores(a, p, qs, kx, low, s_scr, e_scr, inv_scr):
    start = pl.multiple_of(p * BLOCK, BLOCK)
    q = qs[a, p]
    top = jnp.full((8, 2 * BLOCK), NEG_FILL, F32)
    row = lax.broadcasted_iota(jnp.int32, (BLOCK, 2 * BLOCK), 0)
    col = lax.broadcasted_iota(jnp.int32, (BLOCK, 2 * BLOCK), 1) % BLOCK
    for t in range(SPAN // TILE):
        s = dot(kx[a, pl.ds(start + t * TILE, TILE), :], q, NT)
        for u in range(TILE // BLOCK):
            tile = t * (TILE // BLOCK) + u
            ok = row >= low[tile, pl.ds(p, 1), :]
            if tile == WINDOW // BLOCK:
                ok = ok & (row <= col)
            part = jnp.where(ok, s[u * BLOCK : (u + 1) * BLOCK], NEG_FILL)
            s_scr[tile * BLOCK : (tile + 1) * BLOCK, :] = part
            top = jnp.maximum(top, jnp.max(part.reshape(BLOCK // 8, 8, 2 * BLOCK), axis=0))
        yield
    top = jnp.max(top, axis=0, keepdims=True)
    total = jnp.zeros((8, 2 * BLOCK), F32)
    for tile in range(SPAN // BLOCK):
        rows = slice(tile * BLOCK, (tile + 1) * BLOCK)
        e = jnp.exp2((s_scr[rows, :] - top) * EXP2_SCALE)
        total = total + jnp.sum(e.reshape(BLOCK // 8, 8, 2 * BLOCK), axis=0)
        e_scr[rows, :] = e.astype(BF16)
        yield
    inv = 1.0 / jnp.sum(total, axis=0, keepdims=True)
    inv_scr[...] = jnp.broadcast_to(inv, (8, 2 * BLOCK))


def gradients(a, p, qs, gs, kx, vx, kt, vt, out, dq, dk, dv, e_scr, inv_scr, d_scr):
    start = pl.multiple_of(p * BLOCK, BLOCK)
    window = pl.ds(start, SPAN)
    q = qs[a, p]
    inv = inv_scr[0:1, :]
    g_t = (gs[a, p].T.astype(F32) * inv).astype(BF16)
    o_t = (dot(vt[a, :, window], e_scr[...], NN) * inv).astype(BF16)
    delta = jnp.sum(g_t.astype(F32) * o_t.astype(F32), axis=0, keepdims=True)
    out[a, p] = o_t.T
    yield
    for t in range(SPAN // TILE):
        rows = slice(t * TILE, (t + 1) * TILE)
        key_rows = pl.ds(start + t * TILE, TILE)
        e = e_scr[rows, :]
        ds = (e.astype(F32) * (dot(vx[a, key_rows, :], g_t, NN) - delta)).astype(BF16)
        d_scr[rows, :] = ds
        yield
        dv[a, key_rows, :] += dot(e, g_t, NT)
        dk[a, key_rows, :] += dot(ds, q, NN)
        yield
    dq[a, p] = (dot(kt[a, :, window], d_scr[...], NN) * ATTN_SCALE).astype(BF16).T


def interleave(first, second):
    live = True
    while live:
        live = False
        for chunks, times in ((first, 1), (second, 3)):
            for _ in range(times):
                live = next(chunks, chunks) is not chunks or live


def kernel(
    q_ref, k_ref, v_ref, g_ref, band_ref, seg_ref,
    attn_ref, dq_ref, lk, lv, rk, rv,
    qs, gs, kx, vx, kt, vt, low, out, dqs, dk, dv, s_scr, e_0, e_1, inv_0, inv_1, d_scr,
    hk, hv, pk, pv, seg_v, band_v, band_t,
    send, q_in, k_in, v_in, hk_in, hv_in, g_in, o_in, dq_in, rk_in, rv_in, lk_in, lv_in, seg_in, band_in,
):
    me, x = lax.axis_index("ctx"), lax.axis_index("mp")
    chip, core = me // 2, me % 2
    after, before = lax.rem(chip + 1, CHIPS), lax.rem(chip + CHIPS - 1, CHIPS)
    has_after, has_before = chip < CHIPS - 1, chip > 0
    mate = 2 * chip + 1 - core

    barrier = pltpu.get_barrier_semaphore()
    for step in range(1, 2 * X):
        peer = lax.rem(core * X + x + step, 2 * X)
        pl.semaphore_signal(
            barrier, inc=1, device_id=(2 * chip + peer // X, peer % X), device_id_type=MESH
        )
    for other, there in ((after, has_after), (before, has_before)):

        @pl.when(there)
        def _(other=other):
            for c in range(2):
                pl.semaphore_signal(
                    barrier, inc=1, device_id=(2 * other + c, x), device_id_type=MESH
                )


    def push(src, dst, send_at, recv, to):
        pltpu.make_async_remote_copy(
            src_ref=src, dst_ref=dst, send_sem=send.at[send_at], recv_sem=recv,
            device_id=to, device_id_type=MESH,
        ).start()

    def wait(ref, sem):
        pltpu.make_async_copy(ref, ref, sem).wait()

    local_rows = pl.ds(pl.multiple_of(WINDOW + core * 512, 512), 512)
    my_block = core * X + x

    def columns(head):
        return pl.ds(pl.multiple_of(head * HEAD, HEAD), HEAD)

    pltpu.make_async_copy(seg_ref, seg_v, seg_in).start()
    pltpu.make_async_copy(band_ref, band_v, band_in).start()
    neighbours = jnp.minimum(chip, 1) + jnp.minimum(CHIPS - 1 - chip, 1)
    pl.semaphore_wait(barrier, 2 * X - 1 + 2 * neighbours)

    for a in range(2):

        @pl.when(has_after)
        def _(a=a):
            for c in ORDER[a]:
                for b in range(3, -1, -1):
                    rows = slice(b * BLOCK, (b + 1) * BLOCK)
                    to_rows = pl.ds(pl.multiple_of(core * 512 + b * BLOCK, BLOCK), BLOCK)
                    for ref, buf, at, sem in ((k_ref, kx, 0, hk_in), (v_ref, vx, 1, hv_in)):
                        push(
                            ref.at[rows, (2 * c + a) * HEAD : (2 * c + a + 1) * HEAD],
                            buf.at[a, to_rows, :], at, sem.at[a, 4 * core + b], (2 * after + c, x),
                        )

        theirs, mine = 2 * (1 - core) + a, 2 * core + a
        for ref, buf, at, sem in ((k_ref, kx, 2, k_in), (v_ref, vx, 3, v_in)):
            push(ref.at[:, columns(theirs)], buf.at[a, local_rows, :], at, sem.at[a], (mate, x))
            pltpu.make_async_copy(ref.at[:, columns(mine)], buf.at[a, local_rows, :], sem.at[a]).start()
        for g in range(2):
            rows = slice(g * BLOCK, (g + 1) * BLOCK)
            dst = qs.at[a, pl.ds(core * X, X), rows, :]
            push(q_ref.at[:, :, columns(2 * theirs + g)], dst, 4, q_in.at[a], (mate, x))
            pltpu.make_async_copy(q_ref.at[:, :, columns(2 * mine + g)], dst, q_in.at[a]).start()
            dst = gs.at[a, my_block, rows, :]
            pltpu.make_async_copy(
                g_ref.at[:, columns(x * 8 + core * 4 + 2 * a + g)], dst, g_in.at[a]
            ).start()

            def spread(step, carry, dst=dst, a=a, g=g):
                peer = lax.rem(my_block + step, 2 * X)
                c, to_x = peer // X, peer % X
                push(
                    g_ref.at[:, columns(to_x * 8 + c * 4 + 2 * a + g)], dst, 5, g_in.at[a],
                    (2 * chip + c, to_x),
                )
                return carry

            lax.fori_loop(1, 2 * X, spread, 0)

    wait(seg_v, seg_in)
    wait(band_v, band_in)
    seg = seg_v[pl.ds(pl.multiple_of(8 * chip, 8), 8), :]
    every = seg_v[...]
    begin = jnp.zeros((8, BLOCK), jnp.int32)
    for s in range(1, 16):
        count = jnp.sum((every < s).astype(jnp.int32), axis=0, keepdims=True)
        count = jnp.sum(count, axis=1, keepdims=True)
        begin = jnp.maximum(begin, jnp.where(seg >= s, count, 0))
    block = lax.broadcasted_iota(jnp.int32, (8, BLOCK), 0)
    lane = lax.broadcasted_iota(jnp.int32, (8, BLOCK), 1)
    first = jnp.maximum(begin - (chip - 1) * WINDOW, block * BLOCK + lane + 1)
    bands = jnp.concatenate([band_v[...], jnp.zeros((7, 128), jnp.int32)], axis=0)
    band_t[...] = bands.T
    bands = band_t[pl.ds(pl.multiple_of(8 * chip, 8), 8), :]
    for tile in range(SPAN // BLOCK):
        o = WINDOW // BLOCK - tile
        value = first - (block + tile) * BLOCK + (1 - bands[:, o : o + 1]) * FAR
        low[tile] = jnp.concatenate([value, value], axis=1)

    def turn(a, b):
        rows = pl.ds(pl.multiple_of(b * BLOCK, BLOCK), BLOCK)
        kt[a, :, rows] = kx[a, rows, :].T
        vt[a, :, rows] = vx[a, rows, :].T

    def turn_local(i, carry):
        turn(i // 8, 8 + i % 8)
        return carry

    def block_of(i):
        r = i % 8
        return (r + 5) % 8 + (2 - 2 * r) * (1 - (r + 5) // 8)

    def take_halo(a, b):
        rows = pl.ds(pl.multiple_of(b * BLOCK, BLOCK), BLOCK)

        @pl.when(has_before)
        def _():
            wait(kx.at[a, rows, :], hk_in.at[a, b])
            wait(vx.at[a, rows, :], hv_in.at[a, b])

        turn(a, b)

    def score_inputs(i):
        a, r = i // 8, i % 8

        @pl.when(r < 3)
        def _():
            take_halo(a, 7 - r)

        @pl.when(r == 3)
        def _():
            def step(b, carry):
                take_halo(a, 4 - b)
                return carry

            lax.fori_loop(0, 5, step, 0)

    @pl.when(chip == 0)
    def _():
        for a in range(2):
            kx[a, :WINDOW, :] = jnp.zeros((WINDOW, HEAD), BF16)
            vx[a, :WINDOW, :] = jnp.zeros((WINDOW, HEAD), BF16)

    @pl.when(chip == CHIPS - 1)
    def _():
        rk[...] = jnp.zeros_like(rk)
        rv[...] = jnp.zeros_like(rv)

    dk[...] = jnp.zeros_like(dk)
    dv[...] = jnp.zeros_like(dv)
    for a in range(2):
        wait(kx.at[a, WINDOW:, :], k_in.at[a])
        wait(vx.at[a, WINDOW:, :], v_in.at[a])
        wait(qs.at[a], q_in.at[a])
    lax.fori_loop(0, 16, turn_local, 0)
    e_scr, inv_scr = (e_0, e_1), (inv_0, inv_1)

    def score(i, slot):
        return scores(i // 8, block_of(i), qs, kx, low, s_scr, e_scr[slot], inv_scr[slot])

    def grad(i, slot):
        return gradients(
            i // 8, block_of(i), qs, gs, kx, vx, kt, vt, out, dqs, dk, dv, e_scr[slot], inv_scr[slot], d_scr
        )

    def deliver(i):
        a, r, p = i // 8, i % 8, block_of(i)
        head = 2 * core + a

        def give(b, carry):
            rows = pl.ds(pl.multiple_of(b * BLOCK, BLOCK), BLOCK)
            hk[a, b] = (dk[a, rows, :] * ATTN_SCALE).astype(BF16)
            hv[a, b] = dv[a, rows, :].astype(BF16)
            at_rows = pl.ds(pl.multiple_of((b % 4) * BLOCK, BLOCK), BLOCK)
            to = (2 * before + b // 4, x)
            push(hk.at[a, b], rk.at[head, at_rows, :], 6, rk_in.at[head], to)
            push(hv.at[a, b], rv.at[head, at_rows, :], 7, rv_in.at[head], to)
            return carry

        @pl.when(has_before & (r >= 3))
        def _():
            give(p, 0)

        @pl.when(has_before & (r == 7))
        def _():
            lax.fori_loop(5, 8, give, 0)

        for g in range(2):
            part = slice(g * BLOCK, (g + 1) * BLOCK)
            src = out.at[a, p, part, :]
            dst = attn_ref.at[:, columns(x * 8 + core * 4 + 2 * a + g)]

            @pl.when(p == my_block)
            def _():
                pltpu.make_async_copy(src, dst, o_in).start()

            @pl.when(p != my_block)
            def _():
                push(src, dst, 8, o_in, (2 * chip + p // 4, p % 4))

            src2 = dqs.at[a, p, part, :]
            dst2 = dq_ref.at[p % 4, :, columns(2 * head + g)]

            @pl.when(p // 4 == core)
            def _():
                pltpu.make_async_copy(src2, dst2, dq_in).start()

            @pl.when(p // 4 != core)
            def _():
                push(src2, dst2, 9, dq_in, (mate, x))

        @pl.when(r == 7)
        def _():
            theirs = pl.ds(pl.multiple_of(WINDOW + (1 - core) * 512, 512), 512)
            pk[a] = (dk[a, theirs, :] * ATTN_SCALE).astype(BF16)
            pv[a] = dv[a, theirs, :].astype(BF16)
            push(pk.at[a], lk.at[head], 10, lk_in.at[a], (mate, x))
            push(pv.at[a], lv.at[head], 11, lv_in.at[a], (mate, x))
            lk[head] = (dk[a, local_rows, :] * ATTN_SCALE).astype(BF16)
            lv[head] = dv[a, local_rows, :].astype(BF16)

    score_inputs(jnp.int32(0))
    for _ in score(jnp.int32(0), 0):
        pass
    wait(gs.at[0], g_in.at[0])

    def loop(j, carry):
        score_inputs(2 * j + 1)
        interleave(grad(2 * j, 0), score(2 * j + 1, 1))
        deliver(2 * j)

        @pl.when(j == 3)
        def _():
            wait(gs.at[1], g_in.at[1])

        @pl.when(j < 7)
        def _():
            score_inputs(2 * j + 2)

        interleave(grad(2 * j + 1, 1), score(jnp.minimum(2 * j + 2, 15), 0))
        deliver(2 * j + 1)
        return carry

    lax.fori_loop(0, 8, loop, 0)

    for a in range(2):
        wait(lk.at[0], lk_in.at[a])
        wait(lv.at[0], lv_in.at[a])

    @pl.when(has_after)
    def _():
        for h in range(4):
            wait(rk.at[h], rk_in.at[h])
            wait(rv.at[h], rv_in.at[h])
        wait(k_ref, send.at[0])
        wait(v_ref, send.at[1])

    @pl.when(has_before)
    def _():
        wait(hk, send.at[6])
        wait(hv, send.at[7])

    wait(attn_ref, o_in)
    wait(dq_ref, dq_in)
    wait(k_ref.at[:, : 2 * HEAD], send.at[2])
    wait(v_ref.at[:, : 2 * HEAD], send.at[3])
    wait(q_ref.at[:, :, : 4 * HEAD], send.at[4])
    wait(g_ref.at[:, : 28 * HEAD], send.at[5])
    wait(out.at[:, :7], send.at[8])
    wait(dqs.at[:, :4], send.at[9])
    wait(pk, send.at[10])
    wait(pv, send.at[11])


def finish(attn_ref, dq_ref, lk, lv, rk, rv, attn_out, dq_out, dk_out, dv_out, dk, dv, sems):
    copies = [
        pltpu.make_async_copy(attn_ref, attn_out, sems.at[0]),
        pltpu.make_async_copy(dq_ref, dq_out, sems.at[1]),
        pltpu.make_async_copy(dk, dk_out, sems.at[2]),
        pltpu.make_async_copy(dv, dv_out, sems.at[3]),
    ]
    copies[0].start()
    copies[1].start()
    for ours, other, total, copy in ((lk, rk, dk, copies[2]), (lv, rv, dv, copies[3])):
        for h in range(4):
            cols = slice(h * HEAD, (h + 1) * HEAD)
            total[:, cols] = (ours[h].astype(F32) + other[h].astype(F32)).astype(BF16)
        copy.start()
    for copy in copies:
        copy.wait()


def body(queries, keys, values, grad_out, band_mask, segment_ids):
    hbm = pl.BlockSpec(memory_space=pltpu.HBM)
    anywhere = pl.BlockSpec(memory_space=pl.ANY)
    vmem = pl.BlockSpec(memory_space=pltpu.VMEM)
    dma = pltpu.SemaphoreType.DMA
    attn_shape = jax.ShapeDtypeStruct((128, 4096), BF16)
    dq_shape = jax.ShapeDtypeStruct((4, 128, 1024), BF16)
    part = jax.ShapeDtypeStruct((4, 512, 128), BF16)
    pieces = pl.pallas_call(
        kernel,
        out_shape=(attn_shape, dq_shape, part, part, part, part),
        in_specs=[hbm] * 6,
        out_specs=(anywhere, anywhere, vmem, vmem, vmem, vmem),
        scratch_shapes=[
            pltpu.VMEM((2, 8, 256, 128), BF16),
            pltpu.VMEM((2, 8, 256, 128), BF16),
            pltpu.VMEM((2, 2048, 128), BF16),
            pltpu.VMEM((2, 2048, 128), BF16),
            pltpu.VMEM((2, 128, 2048), BF16),
            pltpu.VMEM((2, 128, 2048), BF16),
            pltpu.VMEM((9, 8, 256), jnp.int32),
            pltpu.VMEM((2, 8, 256, 128), BF16),
            pltpu.VMEM((2, 8, 256, 128), BF16),
            pltpu.VMEM((2, 2048, 128), F32),
            pltpu.VMEM((2, 2048, 128), F32),
            pltpu.VMEM((SPAN, 256), F32),
            pltpu.VMEM((SPAN, 256), BF16),
            pltpu.VMEM((SPAN, 256), BF16),
            pltpu.VMEM((8, 256), F32),
            pltpu.VMEM((8, 256), F32),
            pltpu.VMEM((SPAN, 256), BF16),
            pltpu.VMEM((2, 8, 128, 128), BF16),
            pltpu.VMEM((2, 8, 128, 128), BF16),
            pltpu.VMEM((2, 512, 128), BF16),
            pltpu.VMEM((2, 512, 128), BF16),
            pltpu.VMEM((128, 128), jnp.int32),
            pltpu.VMEM((9, 128), jnp.int32),
            pltpu.VMEM((128, 16), jnp.int32),
            dma((12,)),
            dma((2,)), dma((2,)), dma((2,)), dma((2, 8)), dma((2, 8)), dma((2,)),
            dma(()), dma(()),
            dma((4,)), dma((4,)), dma((2,)), dma((2,)),
            dma(()), dma(()),
        ],
        compiler_params=pltpu.CompilerParams(
            collective_id=0, has_side_effects=True, vmem_limit_bytes=48 << 20
        ),
    )(
        *(
            pltpu.with_memory_space_constraint(array, pltpu.HBM)
            for array in (
                queries.reshape(4, 128, 1024), keys, values, grad_out,
                band_mask.T, segment_ids.reshape(128, 128),
            )
        )
    )
    grad = jax.ShapeDtypeStruct((512, 512), BF16)
    attn, dq, dk, dv = pl.pallas_call(
        finish,
        out_shape=(attn_shape, dq_shape, grad, grad),
        in_specs=[anywhere, anywhere, vmem, vmem, vmem, vmem],
        out_specs=(hbm,) * 4,
        scratch_shapes=[pltpu.VMEM((512, 512), BF16), pltpu.VMEM((512, 512), BF16), dma((4,))],
        compiler_params=pltpu.CompilerParams(vmem_limit_bytes=16 << 20),
    )(*pieces)
    return attn, dq.reshape(512, 1024), dk, dv


def solution(mesh):
    placed = (P("ctx", "mp"), P("ctx", "mp"), P("ctx", "mp"), P(("ctx", "mp"), None), P(), P())
    return jax.shard_map(
        body,
        mesh=mesh,
        in_specs=placed,
        out_specs=(P(("ctx", "mp"), None), P("ctx", "mp"), P("ctx", "mp"), P("ctx", "mp")),
        check_vma=False,
    )
```

```python
import math

import jax
import jax.numpy as jnp
from jax import lax
from jax.experimental import pallas as pl
from jax.experimental.pallas import tpu as pltpu
from jax.sharding import PartitionSpec as P

HEAD = 128
BLOCK = 128
WINDOW = 1024
CHIPS = 16
X = 4
SPAN = WINDOW + BLOCK
TILE = 384
ATTN_SCALE = 168.0 ** (-0.5)
EXP2_SCALE = ATTN_SCALE * math.log2(math.e)
NEG_FILL = -1e30
ORDER = ((1, 0), (1, 0))
FAR = 1 << 20

MESH = pl.DeviceIdType.MESH
F32, BF16 = jnp.float32, jnp.bfloat16
NT = (((1,), (1,)), ((), ()))
NN = (((1,), (0,)), ((), ()))


def dot(a, b, dims):
    return lax.dot_general(a, b, dims, preferred_element_type=F32)


def scores(a, p, qs, kx, low, s_scr, e_scr, inv_scr):
    start = pl.multiple_of(p * BLOCK, BLOCK)
    q = qs[a, p]
    top = jnp.full((8, 2 * BLOCK), NEG_FILL, F32)
    row = lax.broadcasted_iota(jnp.int32, (BLOCK, 2 * BLOCK), 0)
    col = lax.broadcasted_iota(jnp.int32, (BLOCK, 2 * BLOCK), 1) % BLOCK
    for t in range(SPAN // TILE):
        s = dot(kx[a, pl.ds(start + t * TILE, TILE), :], q, NT)
        for u in range(TILE // BLOCK):
            tile = t * (TILE // BLOCK) + u
            ok = row >= low[tile, pl.ds(p, 1), :]
            if tile == WINDOW // BLOCK:
                ok = ok & (row <= col)
            part = jnp.where(ok, s[u * BLOCK : (u + 1) * BLOCK], NEG_FILL)
            s_scr[tile * BLOCK : (tile + 1) * BLOCK, :] = part
            top = jnp.maximum(top, jnp.max(part.reshape(BLOCK // 8, 8, 2 * BLOCK), axis=0))
        yield
    top = jnp.max(top, axis=0, keepdims=True)
    total = jnp.zeros((8, 2 * BLOCK), F32)
    for tile in range(SPAN // BLOCK):
        rows = slice(tile * BLOCK, (tile + 1) * BLOCK)
        e = jnp.exp2((s_scr[rows, :] - top) * EXP2_SCALE)
        total = total + jnp.sum(e.reshape(BLOCK // 8, 8, 2 * BLOCK), axis=0)
        e_scr[rows, :] = e.astype(BF16)
        yield
    inv = 1.0 / jnp.sum(total, axis=0, keepdims=True)
    inv_scr[...] = jnp.broadcast_to(inv, (8, 2 * BLOCK))


def gradients(a, p, qs, gs, kx, vx, kt, vt, out, dq, dk, dv, e_scr, inv_scr, d_scr):
    start = pl.multiple_of(p * BLOCK, BLOCK)
    window = pl.ds(start, SPAN)
    q = qs[a, p]
    inv = inv_scr[0:1, :]
    g_t = (gs[a, p].T.astype(F32) * inv).astype(BF16)
    o_t = (dot(vt[a, :, window], e_scr[...], NN) * inv).astype(BF16)
    delta = jnp.sum(g_t.astype(F32) * o_t.astype(F32), axis=0, keepdims=True)
    out[a, p] = o_t.T
    yield
    for t in range(SPAN // TILE):
        rows = slice(t * TILE, (t + 1) * TILE)
        key_rows = pl.ds(start + t * TILE, TILE)
        e = e_scr[rows, :]
        ds = (e.astype(F32) * (dot(vx[a, key_rows, :], g_t, NN) - delta)).astype(BF16)
        d_scr[rows, :] = ds
        yield
        dv[a, key_rows, :] += dot(e, g_t, NT)
        dk[a, key_rows, :] += dot(ds, q, NN)
        yield
    dq[a, p] = (dot(kt[a, :, window], d_scr[...], NN) * ATTN_SCALE).astype(BF16).T


def interleave(first, second):
    live = True
    while live:
        live = False
        for chunks, times in ((first, 1), (second, 3)):
            for _ in range(times):
                live = next(chunks, chunks) is not chunks or live


def kernel(
    q_ref, k_ref, v_ref, g_ref, band_ref, seg_ref,
    attn_ref, dq_ref, lk, lv, rk, rv,
    qs, gs, kx, vx, kt, vt, low, out, dqs, dk, dv, s_scr, e_0, e_1, inv_0, inv_1, d_scr,
    hk, hv, pk, pv, seg_v, band_v, band_t,
    send, q_in, k_in, v_in, hk_in, hv_in, g_in, o_in, dq_in, rk_in, rv_in, lk_in, lv_in, seg_in, band_in,
):
    me, x = lax.axis_index("ctx"), lax.axis_index("mp")
    chip, core = me // 2, me % 2
    after, before = lax.rem(chip + 1, CHIPS), lax.rem(chip + CHIPS - 1, CHIPS)
    has_after, has_before = chip < CHIPS - 1, chip > 0
    mate = 2 * chip + 1 - core

    barrier = pltpu.get_barrier_semaphore()
    for step in range(1, 2 * X):
        peer = lax.rem(core * X + x + step, 2 * X)
        pl.semaphore_signal(
            barrier, inc=1, device_id=(2 * chip + peer // X, peer % X), device_id_type=MESH
        )
    for other, there in ((after, has_after), (before, has_before)):

        @pl.when(there)
        def _(other=other):
            for c in range(2):
                pl.semaphore_signal(
                    barrier, inc=1, device_id=(2 * other + c, x), device_id_type=MESH
                )


    def push(src, dst, send_at, recv, to):
        pltpu.make_async_remote_copy(
            src_ref=src, dst_ref=dst, send_sem=send.at[send_at], recv_sem=recv,
            device_id=to, device_id_type=MESH,
        ).start()

    def wait(ref, sem):
        pltpu.make_async_copy(ref, ref, sem).wait()

    local_rows = pl.ds(pl.multiple_of(WINDOW + core * 512, 512), 512)
    my_block = core * X + x

    def columns(head):
        return pl.ds(pl.multiple_of(head * HEAD, HEAD), HEAD)

    pltpu.make_async_copy(seg_ref, seg_v, seg_in).start()
    pltpu.make_async_copy(band_ref, band_v, band_in).start()
    neighbours = jnp.minimum(chip, 1) + jnp.minimum(CHIPS - 1 - chip, 1)
    pl.semaphore_wait(barrier, 2 * X - 1 + 2 * neighbours)

    for a in range(2):

        @pl.when(has_after)
        def _(a=a):
            for c in ORDER[a]:
                for b in range(3, -1, -1):
                    rows = slice(b * BLOCK, (b + 1) * BLOCK)
                    to_rows = pl.ds(pl.multiple_of(core * 512 + b * BLOCK, BLOCK), BLOCK)
                    for ref, buf, at, sem in ((k_ref, kx, 0, hk_in), (v_ref, vx, 1, hv_in)):
                        push(
                            ref.at[rows, (2 * c + a) * HEAD : (2 * c + a + 1) * HEAD],
                            buf.at[a, to_rows, :], at, sem.at[a, 4 * core + b], (2 * after + c, x),
                        )

        theirs, mine = 2 * (1 - core) + a, 2 * core + a
        for ref, buf, at, sem in ((k_ref, kx, 2, k_in), (v_ref, vx, 3, v_in)):
            push(ref.at[:, columns(theirs)], buf.at[a, local_rows, :], at, sem.at[a], (mate, x))
            pltpu.make_async_copy(ref.at[:, columns(mine)], buf.at[a, local_rows, :], sem.at[a]).start()
        for g in range(2):
            rows = slice(g * BLOCK, (g + 1) * BLOCK)
            dst = qs.at[a, pl.ds(core * X, X), rows, :]
            push(q_ref.at[:, :, columns(2 * theirs + g)], dst, 4, q_in.at[a], (mate, x))
            pltpu.make_async_copy(q_ref.at[:, :, columns(2 * mine + g)], dst, q_in.at[a]).start()
            dst = gs.at[a, my_block, rows, :]
            pltpu.make_async_copy(
                g_ref.at[:, columns(x * 8 + core * 4 + 2 * a + g)], dst, g_in.at[a]
            ).start()

            def spread(step, carry, dst=dst, a=a, g=g):
                peer = lax.rem(my_block + step, 2 * X)
                c, to_x = peer // X, peer % X
                push(
                    g_ref.at[:, columns(to_x * 8 + c * 4 + 2 * a + g)], dst, 5, g_in.at[a],
                    (2 * chip + c, to_x),
                )
                return carry

            lax.fori_loop(1, 2 * X, spread, 0)

    wait(seg_v, seg_in)
    wait(band_v, band_in)
    seg = seg_v[pl.ds(pl.multiple_of(8 * chip, 8), 8), :]
    every = seg_v[...]
    begin = jnp.zeros((8, BLOCK), jnp.int32)
    for s in range(1, 16):
        count = jnp.sum((every < s).astype(jnp.int32), axis=0, keepdims=True)
        count = jnp.sum(count, axis=1, keepdims=True)
        begin = jnp.maximum(begin, jnp.where(seg >= s, count, 0))
    block = lax.broadcasted_iota(jnp.int32, (8, BLOCK), 0)
    lane = lax.broadcasted_iota(jnp.int32, (8, BLOCK), 1)
    first = jnp.maximum(begin - (chip - 1) * WINDOW, block * BLOCK + lane + 1)
    bands = jnp.concatenate([band_v[...], jnp.zeros((7, 128), jnp.int32)], axis=0)
    band_t[...] = bands.T
    bands = band_t[pl.ds(pl.multiple_of(8 * chip, 8), 8), :]
    for tile in range(SPAN // BLOCK):
        o = WINDOW // BLOCK - tile
        value = first - (block + tile) * BLOCK + (1 - bands[:, o : o + 1]) * FAR
        low[tile] = jnp.concatenate([value, value], axis=1)

    def turn(a, b):
        rows = pl.ds(pl.multiple_of(b * BLOCK, BLOCK), BLOCK)
        kt[a, :, rows] = kx[a, rows, :].T
        vt[a, :, rows] = vx[a, rows, :].T

    def turn_local(i, carry):
        turn(i // 8, 8 + i % 8)
        return carry

    def block_of(i):
        r = i % 8
        return (r + 5) % 8 + (2 - 2 * r) * (1 - (r + 5) // 8)

    def take_halo(a, b):
        rows = pl.ds(pl.multiple_of(b * BLOCK, BLOCK), BLOCK)

        @pl.when(has_before)
        def _():
            wait(kx.at[a, rows, :], hk_in.at[a, b])
            wait(vx.at[a, rows, :], hv_in.at[a, b])

        turn(a, b)

    def score_inputs(i):
        a, r = i // 8, i % 8

        @pl.when(r < 3)
        def _():
            take_halo(a, 7 - r)

        @pl.when(r == 3)
        def _():
            def step(b, carry):
                take_halo(a, 4 - b)
                return carry

            lax.fori_loop(0, 5, step, 0)

    @pl.when(chip == 0)
    def _():
        for a in range(2):
            kx[a, :WINDOW, :] = jnp.zeros((WINDOW, HEAD), BF16)
            vx[a, :WINDOW, :] = jnp.zeros((WINDOW, HEAD), BF16)

    @pl.when(chip == CHIPS - 1)
    def _():
        rk[...] = jnp.zeros_like(rk)
        rv[...] = jnp.zeros_like(rv)

    dk[...] = jnp.zeros_like(dk)
    dv[...] = jnp.zeros_like(dv)
    for a in range(2):
        wait(kx.at[a, WINDOW:, :], k_in.at[a])
        wait(vx.at[a, WINDOW:, :], v_in.at[a])
        wait(qs.at[a], q_in.at[a])
    lax.fori_loop(0, 16, turn_local, 0)
    e_scr, inv_scr = (e_0, e_1), (inv_0, inv_1)

    def score(i, slot):
        return scores(i // 8, block_of(i), qs, kx, low, s_scr, e_scr[slot], inv_scr[slot])

    def grad(i, slot):
        return gradients(
            i // 8, block_of(i), qs, gs, kx, vx, kt, vt, out, dqs, dk, dv, e_scr[slot], inv_scr[slot], d_scr
        )

    def deliver(i):
        a, r, p = i // 8, i % 8, block_of(i)
        head = 2 * core + a

        def give(b, carry):
            rows = pl.ds(pl.multiple_of(b * BLOCK, BLOCK), BLOCK)
            hk[a, b] = (dk[a, rows, :] * ATTN_SCALE).astype(BF16)
            hv[a, b] = dv[a, rows, :].astype(BF16)
            at_rows = pl.ds(pl.multiple_of((b % 4) * BLOCK, BLOCK), BLOCK)
            to = (2 * before + b // 4, x)
            push(hk.at[a, b], rk.at[head, at_rows, :], 6, rk_in.at[head], to)
            push(hv.at[a, b], rv.at[head, at_rows, :], 7, rv_in.at[head], to)
            return carry

        @pl.when(has_before & (r >= 3))
        def _():
            give(p, 0)

        @pl.when(has_before & (r == 7))
        def _():
            lax.fori_loop(5, 8, give, 0)

        for g in range(2):
            part = slice(g * BLOCK, (g + 1) * BLOCK)
            src = out.at[a, p, part, :]
            dst = attn_ref.at[:, columns(x * 8 + core * 4 + 2 * a + g)]

            @pl.when(p == my_block)
            def _():
                pltpu.make_async_copy(src, dst, o_in).start()

            @pl.when(p != my_block)
            def _():
                push(src, dst, 8, o_in, (2 * chip + p // 4, p % 4))

            src2 = dqs.at[a, p, part, :]
            dst2 = dq_ref.at[p % 4, :, columns(2 * head + g)]

            @pl.when(p // 4 == core)
            def _():
                pltpu.make_async_copy(src2, dst2, dq_in).start()

            @pl.when(p // 4 != core)
            def _():
                push(src2, dst2, 9, dq_in, (mate, x))

        @pl.when(r == 7)
        def _():
            theirs = pl.ds(pl.multiple_of(WINDOW + (1 - core) * 512, 512), 512)
            pk[a] = (dk[a, theirs, :] * ATTN_SCALE).astype(BF16)
            pv[a] = dv[a, theirs, :].astype(BF16)
            push(pk.at[a], lk.at[head], 10, lk_in.at[a], (mate, x))
            push(pv.at[a], lv.at[head], 11, lv_in.at[a], (mate, x))
            lk[head] = (dk[a, local_rows, :] * ATTN_SCALE).astype(BF16)
            lv[head] = dv[a, local_rows, :].astype(BF16)

    score_inputs(jnp.int32(0))
    for _ in score(jnp.int32(0), 0):
        pass
    wait(gs.at[0], g_in.at[0])

    def loop(i, carry):
        @pl.when(i < 15)
        def _():
            score_inputs(i + 1)

        @pl.when(i == 7)
        def _():
            wait(gs.at[1], g_in.at[1])

        interleave(grad(i, 0), score(jnp.minimum(i + 1, 15), 1))
        e_0[...] = e_1[...]
        inv_0[...] = inv_1[...]
        deliver(i)
        return carry

    lax.fori_loop(0, 16, loop, 0)

    for a in range(2):
        wait(lk.at[0], lk_in.at[a])
        wait(lv.at[0], lv_in.at[a])

    @pl.when(has_after)
    def _():
        for h in range(4):
            wait(rk.at[h], rk_in.at[h])
            wait(rv.at[h], rv_in.at[h])
        wait(k_ref, send.at[0])
        wait(v_ref, send.at[1])

    @pl.when(has_before)
    def _():
        wait(hk, send.at[6])
        wait(hv, send.at[7])

    wait(attn_ref, o_in)
    wait(dq_ref, dq_in)
    wait(k_ref.at[:, : 2 * HEAD], send.at[2])
    wait(v_ref.at[:, : 2 * HEAD], send.at[3])
    wait(q_ref.at[:, :, : 4 * HEAD], send.at[4])
    wait(g_ref.at[:, : 28 * HEAD], send.at[5])
    wait(out.at[:, :7], send.at[8])
    wait(dqs.at[:, :4], send.at[9])
    wait(pk, send.at[10])
    wait(pv, send.at[11])


def finish(attn_ref, dq_ref, lk, lv, rk, rv, attn_out, dq_out, dk_out, dv_out, dk, dv, sems):
    copies = [
        pltpu.make_async_copy(attn_ref, attn_out, sems.at[0]),
        pltpu.make_async_copy(dq_ref, dq_out, sems.at[1]),
        pltpu.make_async_copy(dk, dk_out, sems.at[2]),
        pltpu.make_async_copy(dv, dv_out, sems.at[3]),
    ]
    copies[0].start()
    copies[1].start()
    for ours, other, total, copy in ((lk, rk, dk, copies[2]), (lv, rv, dv, copies[3])):
        for h in range(4):
            cols = slice(h * HEAD, (h + 1) * HEAD)
            total[:, cols] = (ours[h].astype(F32) + other[h].astype(F32)).astype(BF16)
        copy.start()
    for copy in copies:
        copy.wait()


def body(queries, keys, values, grad_out, band_mask, segment_ids):
    hbm = pl.BlockSpec(memory_space=pltpu.HBM)
    anywhere = pl.BlockSpec(memory_space=pl.ANY)
    vmem = pl.BlockSpec(memory_space=pltpu.VMEM)
    dma = pltpu.SemaphoreType.DMA
    attn_shape = jax.ShapeDtypeStruct((128, 4096), BF16)
    dq_shape = jax.ShapeDtypeStruct((4, 128, 1024), BF16)
    part = jax.ShapeDtypeStruct((4, 512, 128), BF16)
    pieces = pl.pallas_call(
        kernel,
        out_shape=(attn_shape, dq_shape, part, part, part, part),
        in_specs=[hbm] * 6,
        out_specs=(anywhere, anywhere, vmem, vmem, vmem, vmem),
        scratch_shapes=[
            pltpu.VMEM((2, 8, 256, 128), BF16),
            pltpu.VMEM((2, 8, 256, 128), BF16),
            pltpu.VMEM((2, 2048, 128), BF16),
            pltpu.VMEM((2, 2048, 128), BF16),
            pltpu.VMEM((2, 128, 2048), BF16),
            pltpu.VMEM((2, 128, 2048), BF16),
            pltpu.VMEM((9, 8, 256), jnp.int32),
            pltpu.VMEM((2, 8, 256, 128), BF16),
            pltpu.VMEM((2, 8, 256, 128), BF16),
            pltpu.VMEM((2, 2048, 128), F32),
            pltpu.VMEM((2, 2048, 128), F32),
            pltpu.VMEM((SPAN, 256), F32),
            pltpu.VMEM((SPAN, 256), BF16),
            pltpu.VMEM((SPAN, 256), BF16),
            pltpu.VMEM((8, 256), F32),
            pltpu.VMEM((8, 256), F32),
            pltpu.VMEM((SPAN, 256), BF16),
            pltpu.VMEM((2, 8, 128, 128), BF16),
            pltpu.VMEM((2, 8, 128, 128), BF16),
            pltpu.VMEM((2, 512, 128), BF16),
            pltpu.VMEM((2, 512, 128), BF16),
            pltpu.VMEM((128, 128), jnp.int32),
            pltpu.VMEM((9, 128), jnp.int32),
            pltpu.VMEM((128, 16), jnp.int32),
            dma((12,)),
            dma((2,)), dma((2,)), dma((2,)), dma((2, 8)), dma((2, 8)), dma((2,)),
            dma(()), dma(()),
            dma((4,)), dma((4,)), dma((2,)), dma((2,)),
            dma(()), dma(()),
        ],
        compiler_params=pltpu.CompilerParams(
            collective_id=0, has_side_effects=True, vmem_limit_bytes=48 << 20
        ),
    )(
        *(
            pltpu.with_memory_space_constraint(array, pltpu.HBM)
            for array in (
                queries.reshape(4, 128, 1024), keys, values, grad_out,
                band_mask.T, segment_ids.reshape(128, 128),
            )
        )
    )
    grad = jax.ShapeDtypeStruct((512, 512), BF16)
    attn, dq, dk, dv = pl.pallas_call(
        finish,
        out_shape=(attn_shape, dq_shape, grad, grad),
        in_specs=[anywhere, anywhere, vmem, vmem, vmem, vmem],
        out_specs=(hbm,) * 4,
        scratch_shapes=[pltpu.VMEM((512, 512), BF16), pltpu.VMEM((512, 512), BF16), dma((4,))],
        compiler_params=pltpu.CompilerParams(vmem_limit_bytes=16 << 20),
    )(*pieces)
    return attn, dq.reshape(512, 1024), dk, dv


def solution(mesh):
    placed = (P("ctx", "mp"), P("ctx", "mp"), P("ctx", "mp"), P(("ctx", "mp"), None), P(), P())
    return jax.shard_map(
        body,
        mesh=mesh,
        in_specs=placed,
        out_specs=(P(("ctx", "mp"), None), P("ctx", "mp"), P("ctx", "mp"), P("ctx", "mp")),
        check_vma=False,
    )
```

```python
import math

import jax
import jax.numpy as jnp
from jax import lax
from jax.experimental import pallas as pl
from jax.experimental.pallas import tpu as pltpu
from jax.sharding import PartitionSpec as P

HEAD = 128
BLOCK = 128
WINDOW = 1024
CHIPS = 16
X = 4
SPAN = WINDOW + BLOCK
TILE = 384
ATTN_SCALE = 168.0 ** (-0.5)
EXP2_SCALE = ATTN_SCALE * math.log2(math.e)
NEG_FILL = -1e30
ORDER = ((1, 0), (1, 0))
FAR = 1 << 20

MESH = pl.DeviceIdType.MESH
F32, BF16 = jnp.float32, jnp.bfloat16
NT = (((1,), (1,)), ((), ()))
NN = (((1,), (0,)), ((), ()))


def dot(a, b, dims):
    return lax.dot_general(a, b, dims, preferred_element_type=F32)


def scores(a, p, qs, kx, low, s_scr, e_scr, inv_scr):
    start = pl.multiple_of(p * BLOCK, BLOCK)
    q = qs[a, p]
    top = jnp.full((8, 2 * BLOCK), NEG_FILL, F32)
    row = lax.broadcasted_iota(jnp.int32, (BLOCK, 2 * BLOCK), 0)
    col = lax.broadcasted_iota(jnp.int32, (BLOCK, 2 * BLOCK), 1) % BLOCK
    for t in range(SPAN // TILE):
        s = dot(kx[a, pl.ds(start + t * TILE, TILE), :], q, NT)
        for u in range(TILE // BLOCK):
            tile = t * (TILE // BLOCK) + u
            ok = row >= low[tile, pl.ds(p, 1), :]
            if tile == WINDOW // BLOCK:
                ok = ok & (row <= col)
            part = jnp.where(ok, s[u * BLOCK : (u + 1) * BLOCK], NEG_FILL)
            s_scr[tile * BLOCK : (tile + 1) * BLOCK, :] = part
            top = jnp.maximum(top, jnp.max(part.reshape(BLOCK // 8, 8, 2 * BLOCK), axis=0))
        yield
    top = jnp.max(top, axis=0, keepdims=True)
    total = jnp.zeros((8, 2 * BLOCK), F32)
    for tile in range(SPAN // BLOCK):
        rows = slice(tile * BLOCK, (tile + 1) * BLOCK)
        e = jnp.exp2((s_scr[rows, :] - top) * EXP2_SCALE)
        total = total + jnp.sum(e.reshape(BLOCK // 8, 8, 2 * BLOCK), axis=0)
        e_scr[rows, :] = e.astype(BF16)
        yield
    inv = 1.0 / jnp.sum(total, axis=0, keepdims=True)
    inv_scr[...] = jnp.broadcast_to(inv, (8, 2 * BLOCK))


def gradients(a, p, qs, gs, kx, vx, kt, vt, out, dq, dk, dv, e_scr, inv_scr, d_scr):
    start = pl.multiple_of(p * BLOCK, BLOCK)
    window = pl.ds(start, SPAN)
    q = qs[a, p]
    inv = inv_scr[0:1, :]
    g_t = (gs[a, p].T.astype(F32) * inv).astype(BF16)
    o_t = (dot(vt[a, :, window], e_scr[...], NN) * inv).astype(BF16)
    delta = jnp.sum(g_t.astype(F32) * o_t.astype(F32), axis=0, keepdims=True)
    out[a, p] = o_t.T.reshape(2, BLOCK, HEAD)
    yield
    for t in range(SPAN // TILE):
        rows = slice(t * TILE, (t + 1) * TILE)
        key_rows = pl.ds(start + t * TILE, TILE)
        e = e_scr[rows, :]
        ds = (e.astype(F32) * (dot(vx[a, key_rows, :], g_t, NN) - delta)).astype(BF16)
        d_scr[rows, :] = ds
        yield
        dv[a, key_rows, :] += dot(e, g_t, NT)
        dk[a, key_rows, :] += dot(ds, q, NN)
        yield
    grad_q = (dot(kt[a, :, window], d_scr[...], NN) * ATTN_SCALE).astype(BF16).T
    dq[a, p] = grad_q.reshape(2, BLOCK, HEAD)


def interleave(first, second):
    live = True
    while live:
        live = False
        for chunks, times in ((first, 1), (second, 4)):
            for _ in range(times):
                live = next(chunks, chunks) is not chunks or live


def kernel(
    q_ref, k_ref, v_ref, g_ref, band_ref, seg_ref,
    attn_ref, dq_ref, lk, lv, rkv,
    qs, gs, kx, vx, kt, vt, low, out, dqs, dk, dv, s_scr, e_0, e_1, inv_0, inv_1, d_scr,
    hkv, pk, pv, seg_v, band_v, band_t,
    send, q_in, k_in, v_in, hk_in, hv_in, g_in, o_in, dq_in, rkv_in, lk_in, lv_in, seg_in, band_in,
):
    me, x = lax.axis_index("ctx"), lax.axis_index("mp")
    chip, core = me // 2, me % 2
    after, before = lax.rem(chip + 1, CHIPS), lax.rem(chip + CHIPS - 1, CHIPS)
    has_after, has_before = chip < CHIPS - 1, chip > 0
    mate = 2 * chip + 1 - core

    barrier = pltpu.get_barrier_semaphore()
    for step in range(1, 2 * X):
        peer = lax.rem(core * X + x + step, 2 * X)
        pl.semaphore_signal(
            barrier, inc=1, device_id=(2 * chip + peer // X, peer % X), device_id_type=MESH
        )
    for other, there in ((after, has_after), (before, has_before)):

        @pl.when(there)
        def _(other=other):
            for c in range(2):
                pl.semaphore_signal(
                    barrier, inc=1, device_id=(2 * other + c, x), device_id_type=MESH
                )


    def push(src, dst, send_at, recv, to):
        pltpu.make_async_remote_copy(
            src_ref=src, dst_ref=dst, send_sem=send.at[send_at], recv_sem=recv,
            device_id=to, device_id_type=MESH,
        ).start()

    def wait(ref, sem):
        pltpu.make_async_copy(ref, ref, sem).wait()

    local_rows = pl.ds(pl.multiple_of(WINDOW + core * 512, 512), 512)
    my_block = core * X + x

    def columns(head):
        return pl.ds(pl.multiple_of(head * HEAD, HEAD), HEAD)

    pltpu.make_async_copy(seg_ref, seg_v, seg_in).start()
    pltpu.make_async_copy(band_ref, band_v, band_in).start()
    neighbours = jnp.minimum(chip, 1) + jnp.minimum(CHIPS - 1 - chip, 1)
    pl.semaphore_wait(barrier, 2 * X - 1 + 2 * neighbours)

    for a in range(2):

        @pl.when(has_after)
        def _(a=a):
            for c in ORDER[a]:
                for b in range(3, -1, -1):
                    rows = slice(b * BLOCK, (b + 1) * BLOCK)
                    to_rows = pl.ds(pl.multiple_of(core * 512 + b * BLOCK, BLOCK), BLOCK)
                    for ref, buf, at, sem in ((k_ref, kx, 0, hk_in), (v_ref, vx, 1, hv_in)):
                        push(
                            ref.at[rows, (2 * c + a) * HEAD : (2 * c + a + 1) * HEAD],
                            buf.at[a, to_rows, :], at, sem.at[a, 4 * core + b], (2 * after + c, x),
                        )

        theirs, mine = 2 * (1 - core) + a, 2 * core + a
        for ref, buf, at, sem in ((k_ref, kx, 2, k_in), (v_ref, vx, 3, v_in)):
            push(ref.at[:, columns(theirs)], buf.at[a, local_rows, :], at, sem.at[a], (mate, x))
            pltpu.make_async_copy(ref.at[:, columns(mine)], buf.at[a, local_rows, :], sem.at[a]).start()
        for g in range(2):
            rows = slice(g * BLOCK, (g + 1) * BLOCK)
            dst = qs.at[a, pl.ds(core * X, X), rows, :]
            push(q_ref.at[:, :, columns(2 * theirs + g)], dst, 4, q_in.at[a], (mate, x))
            pltpu.make_async_copy(q_ref.at[:, :, columns(2 * mine + g)], dst, q_in.at[a]).start()
            dst = gs.at[a, my_block, rows, :]
            pltpu.make_async_copy(
                g_ref.at[:, columns(x * 8 + core * 4 + 2 * a + g)], dst, g_in.at[a]
            ).start()

            def spread(step, carry, dst=dst, a=a, g=g):
                peer = lax.rem(my_block + step, 2 * X)
                c, to_x = peer // X, peer % X
                push(
                    g_ref.at[:, columns(to_x * 8 + c * 4 + 2 * a + g)], dst, 5, g_in.at[a],
                    (2 * chip + c, to_x),
                )
                return carry

            lax.fori_loop(1, 2 * X, spread, 0)

    wait(seg_v, seg_in)
    wait(band_v, band_in)
    seg = seg_v[pl.ds(pl.multiple_of(8 * chip, 8), 8), :]
    every = seg_v[...]
    begin = jnp.zeros((8, BLOCK), jnp.int32)
    for s in range(1, 16):
        count = jnp.sum((every < s).astype(jnp.int32), axis=0, keepdims=True)
        count = jnp.sum(count, axis=1, keepdims=True)
        begin = jnp.maximum(begin, jnp.where(seg >= s, count, 0))
    block = lax.broadcasted_iota(jnp.int32, (8, BLOCK), 0)
    lane = lax.broadcasted_iota(jnp.int32, (8, BLOCK), 1)
    first = jnp.maximum(begin - (chip - 1) * WINDOW, block * BLOCK + lane + 1)
    bands = jnp.concatenate([band_v[...], jnp.zeros((7, 128), jnp.int32)], axis=0)
    band_t[...] = bands.T
    bands = band_t[pl.ds(pl.multiple_of(8 * chip, 8), 8), :]
    for tile in range(SPAN // BLOCK):
        o = WINDOW // BLOCK - tile
        value = first - (block + tile) * BLOCK + (1 - bands[:, o : o + 1]) * FAR
        low[tile] = jnp.concatenate([value, value], axis=1)

    def turn(a, b):
        rows = pl.ds(pl.multiple_of(b * BLOCK, BLOCK), BLOCK)
        kt[a, :, rows] = kx[a, rows, :].T
        vt[a, :, rows] = vx[a, rows, :].T

    def turn_local(i, carry):
        turn(i // 8, 8 + i % 8)
        return carry

    def block_of(i):
        r = i % 8
        return (r + 6) % 8 + (1 - 2 * r) * (1 - (r + 6) // 8)

    def take_halo(a, b):
        rows = pl.ds(pl.multiple_of(b * BLOCK, BLOCK), BLOCK)

        @pl.when(has_before)
        def _():
            wait(kx.at[a, rows, :], hk_in.at[a, b])
            wait(vx.at[a, rows, :], hv_in.at[a, b])

        turn(a, b)

    def score_inputs(i):
        a, r = i // 8, i % 8

        @pl.when(r < 2)
        def _():
            take_halo(a, 7 - r)

        @pl.when(r == 2)
        def _():
            def step(b, carry):
                take_halo(a, 5 - b)
                return carry

            lax.fori_loop(0, 6, step, 0)

    @pl.when(chip == 0)
    def _():
        for a in range(2):
            kx[a, :WINDOW, :] = jnp.zeros((WINDOW, HEAD), BF16)
            vx[a, :WINDOW, :] = jnp.zeros((WINDOW, HEAD), BF16)

    @pl.when(chip == CHIPS - 1)
    def _():
        rkv[...] = jnp.zeros_like(rkv)

    dk[...] = jnp.zeros_like(dk)
    dv[...] = jnp.zeros_like(dv)
    for a in range(2):
        wait(kx.at[a, WINDOW:, :], k_in.at[a])
        wait(vx.at[a, WINDOW:, :], v_in.at[a])
        wait(qs.at[a], q_in.at[a])
    lax.fori_loop(0, 16, turn_local, 0)
    e_scr, inv_scr = (e_0, e_1), (inv_0, inv_1)

    def score(i, slot):
        return scores(i // 8, block_of(i), qs, kx, low, s_scr, e_scr[slot], inv_scr[slot])

    def grad(i, slot):
        return gradients(
            i // 8, block_of(i), qs, gs, kx, vx, kt, vt, out, dqs, dk, dv, e_scr[slot], inv_scr[slot], d_scr
        )

    def deliver(i):
        a, r, p = i // 8, i % 8, block_of(i)
        head = 2 * core + a

        def give(b, carry):
            rows = pl.ds(pl.multiple_of(b * BLOCK, BLOCK), BLOCK)
            hkv[a, b, 0] = (dk[a, rows, :] * ATTN_SCALE).astype(BF16)
            hkv[a, b, 1] = dv[a, rows, :].astype(BF16)
            to = (2 * before + b // 4, x)
            push(hkv.at[a, b], rkv.at[head, b % 4], 6, rkv_in.at[head], to)
            return carry

        @pl.when(has_before & (r >= 2))
        def _():
            give(p, 0)

        @pl.when(has_before & (r == 7))
        def _():
            lax.fori_loop(6, 8, give, 0)

        src = out.at[a, p]
        dst = attn_ref.at[pl.ds(x * 8 + core * 4 + 2 * a, 2)]

        @pl.when(p == my_block)
        def _():
            pltpu.make_async_copy(src, dst, o_in).start()

        @pl.when(p != my_block)
        def _():
            push(src, dst, 8, o_in, (2 * chip + p // 4, p % 4))

        src2 = dqs.at[a, p]
        dst2 = dq_ref.at[pl.ds(2 * head, 2), p % 4]

        @pl.when(p // 4 == core)
        def _():
            pltpu.make_async_copy(src2, dst2, dq_in).start()

        @pl.when(p // 4 != core)
        def _():
            push(src2, dst2, 9, dq_in, (mate, x))

        @pl.when(r == 7)
        def _():
            theirs = pl.ds(pl.multiple_of(WINDOW + (1 - core) * 512, 512), 512)
            pk[a] = (dk[a, theirs, :] * ATTN_SCALE).astype(BF16)
            pv[a] = dv[a, theirs, :].astype(BF16)
            push(pk.at[a], lk.at[head], 10, lk_in.at[a], (mate, x))
            push(pv.at[a], lv.at[head], 11, lv_in.at[a], (mate, x))
            lk[head] = (dk[a, local_rows, :] * ATTN_SCALE).astype(BF16)
            lv[head] = dv[a, local_rows, :].astype(BF16)

    score_inputs(jnp.int32(0))
    for _ in score(jnp.int32(0), 0):
        pass
    wait(gs.at[0], g_in.at[0])

    def loop(i, carry):
        @pl.when(i < 15)
        def _():
            score_inputs(i + 1)

        @pl.when(i == 7)
        def _():
            wait(gs.at[1], g_in.at[1])

        interleave(grad(i, 0), score(jnp.minimum(i + 1, 15), 1))
        e_0[...] = e_1[...]
        inv_0[...] = inv_1[...]
        deliver(i)
        return carry

    lax.fori_loop(0, 16, loop, 0)

    for a in range(2):
        wait(lk.at[0], lk_in.at[a])
        wait(lv.at[0], lv_in.at[a])

    @pl.when(has_after)
    def _():
        for h in range(4):
            wait(rkv.at[h], rkv_in.at[h])
        wait(k_ref, send.at[0])
        wait(v_ref, send.at[1])

    @pl.when(has_before)
    def _():
        wait(hkv, send.at[6])

    wait(attn_ref, o_in)
    wait(dq_ref, dq_in)
    wait(k_ref.at[:, : 2 * HEAD], send.at[2])
    wait(v_ref.at[:, : 2 * HEAD], send.at[3])
    wait(q_ref.at[:, :, : 4 * HEAD], send.at[4])
    wait(g_ref.at[:, : 28 * HEAD], send.at[5])
    wait(out.at[:, :7], send.at[8])
    wait(dqs.at[:, :4], send.at[9])
    wait(pk, send.at[10])
    wait(pv, send.at[11])


def finish(attn_ref, dq_ref, lk, lv, rkv, attn_out, dq_out, dk_out, dv_out, dk, dv, sems):
    for h in range(32):
        cols = slice(h * HEAD, (h + 1) * HEAD)
        pltpu.make_async_copy(attn_ref.at[h], attn_out.at[:, cols], sems.at[0]).start()
    for h in range(8):
        cols = slice(h * HEAD, (h + 1) * HEAD)
        pltpu.make_async_copy(dq_ref.at[h], dq_out.at[:, :, cols], sems.at[1]).start()
    copies = [
        pltpu.make_async_copy(dk, dk_out, sems.at[2]),
        pltpu.make_async_copy(dv, dv_out, sems.at[3]),
    ]
    for which, ours, total in ((0, lk, dk), (1, lv, dv)):
        for h in range(4):
            cols = slice(h * HEAD, (h + 1) * HEAD)
            other = rkv[h, :, which].reshape(4 * BLOCK, HEAD)
            total[:, cols] = (ours[h].astype(F32) + other.astype(F32)).astype(BF16)
        copies[which].start()
    pltpu.make_async_copy(attn_ref, attn_ref, sems.at[0]).wait()
    pltpu.make_async_copy(dq_ref, dq_ref, sems.at[1]).wait()
    for copy in copies:
        copy.wait()


def body(queries, keys, values, grad_out, band_mask, segment_ids):
    hbm = pl.BlockSpec(memory_space=pltpu.HBM)
    anywhere = pl.BlockSpec(memory_space=pl.ANY)
    vmem = pl.BlockSpec(memory_space=pltpu.VMEM)
    dma = pltpu.SemaphoreType.DMA
    part = jax.ShapeDtypeStruct((4, 512, 128), BF16)
    pieces = pl.pallas_call(
        kernel,
        out_shape=(
            jax.ShapeDtypeStruct((32, 128, 128), BF16),
            jax.ShapeDtypeStruct((8, 4, 128, 128), BF16),
            part,
            part,
            jax.ShapeDtypeStruct((4, 4, 2, 128, 128), BF16),
        ),
        in_specs=[hbm] * 6,
        out_specs=(anywhere, anywhere, vmem, vmem, vmem),
        scratch_shapes=[
            pltpu.VMEM((2, 8, 256, 128), BF16),
            pltpu.VMEM((2, 8, 256, 128), BF16),
            pltpu.VMEM((2, 2048, 128), BF16),
            pltpu.VMEM((2, 2048, 128), BF16),
            pltpu.VMEM((2, 128, 2048), BF16),
            pltpu.VMEM((2, 128, 2048), BF16),
            pltpu.VMEM((9, 8, 256), jnp.int32),
            pltpu.VMEM((2, 8, 2, 128, 128), BF16),
            pltpu.VMEM((2, 8, 2, 128, 128), BF16),
            pltpu.VMEM((2, 2048, 128), F32),
            pltpu.VMEM((2, 2048, 128), F32),
            pltpu.VMEM((SPAN, 256), F32),
            pltpu.VMEM((SPAN, 256), BF16),
            pltpu.VMEM((SPAN, 256), BF16),
            pltpu.VMEM((8, 256), F32),
            pltpu.VMEM((8, 256), F32),
            pltpu.VMEM((SPAN, 256), BF16),
            pltpu.VMEM((2, 8, 2, 128, 128), BF16),
            pltpu.VMEM((2, 512, 128), BF16),
            pltpu.VMEM((2, 512, 128), BF16),
            pltpu.VMEM((128, 128), jnp.int32),
            pltpu.VMEM((9, 128), jnp.int32),
            pltpu.VMEM((128, 16), jnp.int32),
            dma((12,)),
            dma((2,)), dma((2,)), dma((2,)), dma((2, 8)), dma((2, 8)), dma((2,)),
            dma(()), dma(()),
            dma((4,)), dma((2,)), dma((2,)),
            dma(()), dma(()),
        ],
        compiler_params=pltpu.CompilerParams(
            collective_id=0, has_side_effects=True, vmem_limit_bytes=48 << 20
        ),
    )(
        *(
            pltpu.with_memory_space_constraint(array, pltpu.HBM)
            for array in (
                queries.reshape(4, 128, 1024), keys, values, grad_out,
                band_mask.T, segment_ids.reshape(128, 128),
            )
        )
    )
    grad = jax.ShapeDtypeStruct((512, 512), BF16)
    attn, dq, dk, dv = pl.pallas_call(
        finish,
        out_shape=(
            jax.ShapeDtypeStruct((128, 4096), BF16),
            jax.ShapeDtypeStruct((4, 128, 1024), BF16),
            grad,
            grad,
        ),
        in_specs=[anywhere, anywhere, vmem, vmem, vmem],
        out_specs=(hbm,) * 4,
        scratch_shapes=[pltpu.VMEM((512, 512), BF16), pltpu.VMEM((512, 512), BF16), dma((4,))],
        compiler_params=pltpu.CompilerParams(vmem_limit_bytes=16 << 20),
    )(*pieces)
    return attn, dq.reshape(512, 1024), dk, dv


def solution(mesh):
    placed = (P("ctx", "mp"), P("ctx", "mp"), P("ctx", "mp"), P(("ctx", "mp"), None), P(), P())
    return jax.shard_map(
        body,
        mesh=mesh,
        in_specs=placed,
        out_specs=(P(("ctx", "mp"), None), P("ctx", "mp"), P("ctx", "mp"), P("ctx", "mp")),
        check_vma=False,
    )
```

```python
import math

import jax
import jax.numpy as jnp
from jax import lax
from jax.experimental import pallas as pl
from jax.experimental.pallas import tpu as pltpu
from jax.sharding import PartitionSpec as P

HEAD = 128
BLOCK = 128
WINDOW = 1024
CHIPS = 16
X = 4
SPAN = WINDOW + BLOCK
TILE = 384
ATTN_SCALE = 168.0 ** (-0.5)
EXP2_SCALE = ATTN_SCALE * math.log2(math.e)
NEG_FILL = -1e30
ORDER = ((1, 0), (1, 0))
FAR = 1 << 20

MESH = pl.DeviceIdType.MESH
F32, BF16 = jnp.float32, jnp.bfloat16
NT = (((1,), (1,)), ((), ()))
NN = (((1,), (0,)), ((), ()))


def dot(a, b, dims):
    return lax.dot_general(a, b, dims, preferred_element_type=F32)


def scores(a, p, qs, kx, low, s_scr, e_scr, inv_scr):
    start = pl.multiple_of(p * BLOCK, BLOCK)
    q = qs[a, p]
    top = jnp.full((8, 2 * BLOCK), NEG_FILL, F32)
    row = lax.broadcasted_iota(jnp.int32, (BLOCK, 2 * BLOCK), 0)
    col = lax.broadcasted_iota(jnp.int32, (BLOCK, 2 * BLOCK), 1) % BLOCK
    for t in range(SPAN // TILE):
        s = dot(kx[a, pl.ds(start + t * TILE, TILE), :], q, NT)
        for u in range(TILE // BLOCK):
            tile = t * (TILE // BLOCK) + u
            ok = row >= low[tile, pl.ds(p, 1), :]
            if tile == WINDOW // BLOCK:
                ok = ok & (row <= col)
            part = jnp.where(ok, s[u * BLOCK : (u + 1) * BLOCK], NEG_FILL)
            s_scr[tile * BLOCK : (tile + 1) * BLOCK, :] = part
            top = jnp.maximum(top, jnp.max(part.reshape(BLOCK // 8, 8, 2 * BLOCK), axis=0))
        yield
    top = jnp.max(top, axis=0, keepdims=True)
    total = jnp.zeros((8, 2 * BLOCK), F32)
    for tile in range(SPAN // BLOCK):
        rows = slice(tile * BLOCK, (tile + 1) * BLOCK)
        e = jnp.exp2((s_scr[rows, :] - top) * EXP2_SCALE)
        total = total + jnp.sum(e.reshape(BLOCK // 8, 8, 2 * BLOCK), axis=0)
        e_scr[rows, :] = e.astype(BF16)
        yield
    inv = 1.0 / jnp.sum(total, axis=0, keepdims=True)
    inv_scr[...] = jnp.broadcast_to(inv, (8, 2 * BLOCK))


def gradients(a, p, qs, gs, kx, vx, kt, vt, out, dq, dk, dv, e_scr, inv_scr, d_scr):
    start = pl.multiple_of(p * BLOCK, BLOCK)
    window = pl.ds(start, SPAN)
    q = qs[a, p]
    inv = inv_scr[0:1, :]
    g_t = (gs[a, p].T.astype(F32) * inv).astype(BF16)
    o_t = (dot(vt[a, :, window], e_scr[...], NN) * inv).astype(BF16)
    delta = jnp.sum(g_t.astype(F32) * o_t.astype(F32), axis=0, keepdims=True)
    out[a, p] = o_t.T.reshape(2, BLOCK, HEAD)
    yield
    for t in range(SPAN // TILE):
        rows = slice(t * TILE, (t + 1) * TILE)
        key_rows = pl.ds(start + t * TILE, TILE)
        e = e_scr[rows, :]
        ds = e * (dot(vx[a, key_rows, :], g_t, NN) - delta).astype(BF16)
        d_scr[rows, :] = ds
        yield
        dv[a, key_rows, :] += dot(e, g_t, NT)
        dk[a, key_rows, :] += dot(ds, q, NN)
        yield
    grad_q = (dot(kt[a, :, window], d_scr[...], NN) * ATTN_SCALE).astype(BF16).T
    dq[a, p] = grad_q.reshape(2, BLOCK, HEAD)


def interleave(first, second):
    live = True
    while live:
        live = False
        for chunks, times in ((first, 1), (second, 4)):
            for _ in range(times):
                live = next(chunks, chunks) is not chunks or live


def kernel(
    q_ref, k_ref, v_ref, g_ref, band_ref, seg_ref,
    attn_ref, dq_ref, lk, lv, rkv,
    qs, gs, kx, vx, kt, vt, low, out, dqs, dk, dv, s_scr, e_0, e_1, inv_0, inv_1, d_scr,
    hkv, pk, pv, seg_v, band_v, band_t,
    send, q_in, k_in, v_in, hk_in, hv_in, g_in, o_in, dq_in, rkv_in, lk_in, lv_in, seg_in, band_in,
):
    me, x = lax.axis_index("ctx"), lax.axis_index("mp")
    chip, core = me // 2, me % 2
    after, before = lax.rem(chip + 1, CHIPS), lax.rem(chip + CHIPS - 1, CHIPS)
    has_after, has_before = chip < CHIPS - 1, chip > 0
    mate = 2 * chip + 1 - core

    barrier = pltpu.get_barrier_semaphore()
    for step in range(1, 2 * X):
        peer = lax.rem(core * X + x + step, 2 * X)
        pl.semaphore_signal(
            barrier, inc=1, device_id=(2 * chip + peer // X, peer % X), device_id_type=MESH
        )
    for other, there in ((after, has_after), (before, has_before)):

        @pl.when(there)
        def _(other=other):
            for c in range(2):
                pl.semaphore_signal(
                    barrier, inc=1, device_id=(2 * other + c, x), device_id_type=MESH
                )


    def push(src, dst, send_at, recv, to):
        pltpu.make_async_remote_copy(
            src_ref=src, dst_ref=dst, send_sem=send.at[send_at], recv_sem=recv,
            device_id=to, device_id_type=MESH,
        ).start()

    def wait(ref, sem):
        pltpu.make_async_copy(ref, ref, sem).wait()

    local_rows = pl.ds(pl.multiple_of(WINDOW + core * 512, 512), 512)
    my_block = core * X + x

    def columns(head):
        return pl.ds(pl.multiple_of(head * HEAD, HEAD), HEAD)

    pltpu.make_async_copy(seg_ref, seg_v, seg_in).start()
    pltpu.make_async_copy(band_ref, band_v, band_in).start()
    neighbours = jnp.minimum(chip, 1) + jnp.minimum(CHIPS - 1 - chip, 1)
    pl.semaphore_wait(barrier, 2 * X - 1 + 2 * neighbours)

    for a in range(2):

        @pl.when(has_after)
        def _(a=a):
            for c in ORDER[a]:
                for b in range(3, -1, -1):
                    rows = slice(b * BLOCK, (b + 1) * BLOCK)
                    to_rows = pl.ds(pl.multiple_of(core * 512 + b * BLOCK, BLOCK), BLOCK)
                    for ref, buf, at, sem in ((k_ref, kx, 0, hk_in), (v_ref, vx, 1, hv_in)):
                        push(
                            ref.at[rows, (2 * c + a) * HEAD : (2 * c + a + 1) * HEAD],
                            buf.at[a, to_rows, :], at, sem.at[a, 4 * core + b], (2 * after + c, x),
                        )

        theirs, mine = 2 * (1 - core) + a, 2 * core + a
        for ref, buf, at, sem in ((k_ref, kx, 2, k_in), (v_ref, vx, 3, v_in)):
            push(ref.at[:, columns(theirs)], buf.at[a, local_rows, :], at, sem.at[a], (mate, x))
            pltpu.make_async_copy(ref.at[:, columns(mine)], buf.at[a, local_rows, :], sem.at[a]).start()
        for g in range(2):
            rows = slice(g * BLOCK, (g + 1) * BLOCK)
            dst = qs.at[a, pl.ds(core * X, X), rows, :]
            push(q_ref.at[:, :, columns(2 * theirs + g)], dst, 4, q_in.at[a], (mate, x))
            pltpu.make_async_copy(q_ref.at[:, :, columns(2 * mine + g)], dst, q_in.at[a]).start()
            dst = gs.at[a, my_block, rows, :]
            pltpu.make_async_copy(
                g_ref.at[:, columns(x * 8 + core * 4 + 2 * a + g)], dst, g_in.at[a]
            ).start()

            def spread(step, carry, dst=dst, a=a, g=g):
                peer = lax.rem(my_block + step, 2 * X)
                c, to_x = peer // X, peer % X
                push(
                    g_ref.at[:, columns(to_x * 8 + c * 4 + 2 * a + g)], dst, 5, g_in.at[a],
                    (2 * chip + c, to_x),
                )
                return carry

            lax.fori_loop(1, 2 * X, spread, 0)

    wait(seg_v, seg_in)
    wait(band_v, band_in)
    seg = seg_v[pl.ds(pl.multiple_of(8 * chip, 8), 8), :]
    every = seg_v[...]
    begin = jnp.zeros((8, BLOCK), jnp.int32)
    for s in range(1, 16):
        count = jnp.sum((every < s).astype(jnp.int32), axis=0, keepdims=True)
        count = jnp.sum(count, axis=1, keepdims=True)
        begin = jnp.maximum(begin, jnp.where(seg >= s, count, 0))
    block = lax.broadcasted_iota(jnp.int32, (8, BLOCK), 0)
    lane = lax.broadcasted_iota(jnp.int32, (8, BLOCK), 1)
    first = jnp.maximum(begin - (chip - 1) * WINDOW, block * BLOCK + lane + 1)
    bands = jnp.concatenate([band_v[...], jnp.zeros((7, 128), jnp.int32)], axis=0)
    band_t[...] = bands.T
    bands = band_t[pl.ds(pl.multiple_of(8 * chip, 8), 8), :]
    for tile in range(SPAN // BLOCK):
        o = WINDOW // BLOCK - tile
        value = first - (block + tile) * BLOCK + (1 - bands[:, o : o + 1]) * FAR
        low[tile] = jnp.concatenate([value, value], axis=1)

    def turn(a, b):
        rows = pl.ds(pl.multiple_of(b * BLOCK, BLOCK), BLOCK)
        kt[a, :, rows] = kx[a, rows, :].T
        vt[a, :, rows] = vx[a, rows, :].T

    def turn_local(i, carry):
        turn(i // 8, 8 + i % 8)
        return carry

    def block_of(i):
        r = i % 8
        return (r + 6) % 8 + (1 - 2 * r) * (1 - (r + 6) // 8)

    def take_halo(a, b):
        rows = pl.ds(pl.multiple_of(b * BLOCK, BLOCK), BLOCK)

        @pl.when(has_before)
        def _():
            wait(kx.at[a, rows, :], hk_in.at[a, b])
            wait(vx.at[a, rows, :], hv_in.at[a, b])

        turn(a, b)

    def score_inputs(i):
        a, r = i // 8, i % 8

        @pl.when(r < 2)
        def _():
            take_halo(a, 7 - r)

        @pl.when(r == 2)
        def _():
            def step(b, carry):
                take_halo(a, 5 - b)
                return carry

            lax.fori_loop(0, 6, step, 0)

    @pl.when(chip == 0)
    def _():
        for a in range(2):
            kx[a, :WINDOW, :] = jnp.zeros((WINDOW, HEAD), BF16)
            vx[a, :WINDOW, :] = jnp.zeros((WINDOW, HEAD), BF16)

    @pl.when(chip == CHIPS - 1)
    def _():
        rkv[...] = jnp.zeros_like(rkv)

    dk[...] = jnp.zeros_like(dk)
    dv[...] = jnp.zeros_like(dv)
    for a in range(2):
        wait(kx.at[a, WINDOW:, :], k_in.at[a])
        wait(vx.at[a, WINDOW:, :], v_in.at[a])
        wait(qs.at[a], q_in.at[a])
    lax.fori_loop(0, 16, turn_local, 0)
    e_scr, inv_scr = (e_0, e_1), (inv_0, inv_1)

    def score(i, slot):
        return scores(i // 8, block_of(i), qs, kx, low, s_scr, e_scr[slot], inv_scr[slot])

    def grad(i, slot):
        return gradients(
            i // 8, block_of(i), qs, gs, kx, vx, kt, vt, out, dqs, dk, dv, e_scr[slot], inv_scr[slot], d_scr
        )

    def deliver(i):
        a, r, p = i // 8, i % 8, block_of(i)
        head = 2 * core + a

        def give(b, carry):
            rows = pl.ds(pl.multiple_of(b * BLOCK, BLOCK), BLOCK)
            hkv[a, b, 0] = (dk[a, rows, :] * ATTN_SCALE).astype(BF16)
            hkv[a, b, 1] = dv[a, rows, :].astype(BF16)
            to = (2 * before + b // 4, x)
            push(hkv.at[a, b], rkv.at[head, b % 4], 6, rkv_in.at[head], to)
            return carry

        @pl.when(has_before & (r >= 2))
        def _():
            give(p, 0)

        @pl.when(has_before & (r == 7))
        def _():
            lax.fori_loop(6, 8, give, 0)

        src = out.at[a, p]
        dst = attn_ref.at[pl.ds(x * 8 + core * 4 + 2 * a, 2)]

        @pl.when(p == my_block)
        def _():
            pltpu.make_async_copy(src, dst, o_in).start()

        @pl.when(p != my_block)
        def _():
            push(src, dst, 8, o_in, (2 * chip + p // 4, p % 4))

        src2 = dqs.at[a, p]
        dst2 = dq_ref.at[pl.ds(2 * head, 2), p % 4]

        @pl.when(p // 4 == core)
        def _():
            pltpu.make_async_copy(src2, dst2, dq_in).start()

        @pl.when(p // 4 != core)
        def _():
            push(src2, dst2, 9, dq_in, (mate, x))

        @pl.when(r == 7)
        def _():
            theirs = pl.ds(pl.multiple_of(WINDOW + (1 - core) * 512, 512), 512)
            pk[a] = (dk[a, theirs, :] * ATTN_SCALE).astype(BF16)
            pv[a] = dv[a, theirs, :].astype(BF16)
            push(pk.at[a], lk.at[head], 10, lk_in.at[a], (mate, x))
            push(pv.at[a], lv.at[head], 11, lv_in.at[a], (mate, x))
            lk[head] = (dk[a, local_rows, :] * ATTN_SCALE).astype(BF16)
            lv[head] = dv[a, local_rows, :].astype(BF16)

    score_inputs(jnp.int32(0))
    for _ in score(jnp.int32(0), 0):
        pass
    wait(gs.at[0], g_in.at[0])

    def loop(i, carry):
        @pl.when(i < 15)
        def _():
            score_inputs(i + 1)

        @pl.when(i == 7)
        def _():
            wait(gs.at[1], g_in.at[1])

        interleave(grad(i, 0), score(jnp.minimum(i + 1, 15), 1))
        e_0[...] = e_1[...]
        inv_0[...] = inv_1[...]
        deliver(i)
        return carry

    lax.fori_loop(0, 16, loop, 0)

    for a in range(2):
        wait(lk.at[0], lk_in.at[a])
        wait(lv.at[0], lv_in.at[a])

    @pl.when(has_after)
    def _():
        for h in range(4):
            wait(rkv.at[h], rkv_in.at[h])
        wait(k_ref, send.at[0])
        wait(v_ref, send.at[1])

    @pl.when(has_before)
    def _():
        wait(hkv, send.at[6])

    wait(attn_ref, o_in)
    wait(dq_ref, dq_in)
    wait(k_ref.at[:, : 2 * HEAD], send.at[2])
    wait(v_ref.at[:, : 2 * HEAD], send.at[3])
    wait(q_ref.at[:, :, : 4 * HEAD], send.at[4])
    wait(g_ref.at[:, : 28 * HEAD], send.at[5])
    wait(out.at[:, :7], send.at[8])
    wait(dqs.at[:, :4], send.at[9])
    wait(pk, send.at[10])
    wait(pv, send.at[11])


def finish(attn_ref, dq_ref, lk, lv, rkv, attn_out, dq_out, dk_out, dv_out, dk, dv, sems):
    for h in range(32):
        cols = slice(h * HEAD, (h + 1) * HEAD)
        pltpu.make_async_copy(attn_ref.at[h], attn_out.at[:, cols], sems.at[0]).start()
    for h in range(8):
        cols = slice(h * HEAD, (h + 1) * HEAD)
        pltpu.make_async_copy(dq_ref.at[h], dq_out.at[:, :, cols], sems.at[1]).start()
    copies = [
        pltpu.make_async_copy(dk, dk_out, sems.at[2]),
        pltpu.make_async_copy(dv, dv_out, sems.at[3]),
    ]
    for which, ours, total in ((0, lk, dk), (1, lv, dv)):
        for h in range(4):
            cols = slice(h * HEAD, (h + 1) * HEAD)
            other = rkv[h, :, which].reshape(4 * BLOCK, HEAD)
            total[:, cols] = (ours[h].astype(F32) + other.astype(F32)).astype(BF16)
        copies[which].start()
    pltpu.make_async_copy(attn_ref, attn_ref, sems.at[0]).wait()
    pltpu.make_async_copy(dq_ref, dq_ref, sems.at[1]).wait()
    for copy in copies:
        copy.wait()


def body(queries, keys, values, grad_out, band_mask, segment_ids):
    hbm = pl.BlockSpec(memory_space=pltpu.HBM)
    anywhere = pl.BlockSpec(memory_space=pl.ANY)
    vmem = pl.BlockSpec(memory_space=pltpu.VMEM)
    dma = pltpu.SemaphoreType.DMA
    part = jax.ShapeDtypeStruct((4, 512, 128), BF16)
    pieces = pl.pallas_call(
        kernel,
        out_shape=(
            jax.ShapeDtypeStruct((32, 128, 128), BF16),
            jax.ShapeDtypeStruct((8, 4, 128, 128), BF16),
            part,
            part,
            jax.ShapeDtypeStruct((4, 4, 2, 128, 128), BF16),
        ),
        in_specs=[hbm] * 6,
        out_specs=(anywhere, anywhere, vmem, vmem, vmem),
        scratch_shapes=[
            pltpu.VMEM((2, 8, 256, 128), BF16),
            pltpu.VMEM((2, 8, 256, 128), BF16),
            pltpu.VMEM((2, 2048, 128), BF16),
            pltpu.VMEM((2, 2048, 128), BF16),
            pltpu.VMEM((2, 128, 2048), BF16),
            pltpu.VMEM((2, 128, 2048), BF16),
            pltpu.VMEM((9, 8, 256), jnp.int32),
            pltpu.VMEM((2, 8, 2, 128, 128), BF16),
            pltpu.VMEM((2, 8, 2, 128, 128), BF16),
            pltpu.VMEM((2, 2048, 128), F32),
            pltpu.VMEM((2, 2048, 128), F32),
            pltpu.VMEM((SPAN, 256), F32),
            pltpu.VMEM((SPAN, 256), BF16),
            pltpu.VMEM((SPAN, 256), BF16),
            pltpu.VMEM((8, 256), F32),
            pltpu.VMEM((8, 256), F32),
            pltpu.VMEM((SPAN, 256), BF16),
            pltpu.VMEM((2, 8, 2, 128, 128), BF16),
            pltpu.VMEM((2, 512, 128), BF16),
            pltpu.VMEM((2, 512, 128), BF16),
            pltpu.VMEM((128, 128), jnp.int32),
            pltpu.VMEM((9, 128), jnp.int32),
            pltpu.VMEM((128, 16), jnp.int32),
            dma((12,)),
            dma((2,)), dma((2,)), dma((2,)), dma((2, 8)), dma((2, 8)), dma((2,)),
            dma(()), dma(()),
            dma((4,)), dma((2,)), dma((2,)),
            dma(()), dma(()),
        ],
        compiler_params=pltpu.CompilerParams(
            collective_id=0, has_side_effects=True, vmem_limit_bytes=48 << 20
        ),
    )(
        *(
            pltpu.with_memory_space_constraint(array, pltpu.HBM)
            for array in (
                queries.reshape(4, 128, 1024), keys, values, grad_out,
                band_mask.T, segment_ids.reshape(128, 128),
            )
        )
    )
    grad = jax.ShapeDtypeStruct((512, 512), BF16)
    attn, dq, dk, dv = pl.pallas_call(
        finish,
        out_shape=(
            jax.ShapeDtypeStruct((128, 4096), BF16),
            jax.ShapeDtypeStruct((4, 128, 1024), BF16),
            grad,
            grad,
        ),
        in_specs=[anywhere, anywhere, vmem, vmem, vmem],
        out_specs=(hbm,) * 4,
        scratch_shapes=[pltpu.VMEM((512, 512), BF16), pltpu.VMEM((512, 512), BF16), dma((4,))],
        compiler_params=pltpu.CompilerParams(vmem_limit_bytes=16 << 20),
    )(*pieces)
    return attn, dq.reshape(512, 1024), dk, dv


def solution(mesh):
    placed = (P("ctx", "mp"), P("ctx", "mp"), P("ctx", "mp"), P(("ctx", "mp"), None), P(), P())
    return jax.shard_map(
        body,
        mesh=mesh,
        in_specs=placed,
        out_specs=(P(("ctx", "mp"), None), P("ctx", "mp"), P("ctx", "mp"), P("ctx", "mp")),
        check_vma=False,
    )
```
